32 devices in a mesh: node: 16 (over z, y, core), chip: 2 (over x).
Axes of the slice: x: 2, y: 2, z: 4, core: 2. Of those that a mesh axis runs over, the one named last changes fastest.
Arguments:
- tokens: bfloat16 [256, 3584], P(('node', 'chip')), may hold values from -6 to 6
- expert_ids: int32 [256, 8], P(('node', 'chip')), may hold values from 0 to 31, as said below
- gate_values: bfloat16 [256, 8], P(('node', 'chip')), may hold values from 0.099609375 to 1
- slot_ids: int32 [256, 8], P(('node', 'chip')), may hold values from 0 to 7, as said below
- up_weight: bfloat16 [32, 3584, 1024], P('node', None, 'chip'), may hold values from -0.09375 to 0.09375
- down_weight: bfloat16 [32, 1024, 3584], P('node', 'chip'), may hold values from -0.1875 to 0.1875
Outputs:
- mixed: bfloat16 [256, 3584], P(('node', 'chip'))
The draws below stay inside these ranges and needn't reach their ends.
Inputs may be any that keep to these rules, and one draw needn't show every extreme that they name: `expert_ids`: each token's 8 entries name, in some order, all 2 experts of each of 4 distinct nodes. `slot_ids`: entries of one token that name experts of the same node hold the same slot; among the 16 tokens of one node (aligned blocks of the token dimension), the slots to one destination node are distinct, and some destination node receives all 8 slots from each source node.
All inputs are finite; a program needn't handle non-finite values.
Results may differ from the reference program's by a relative error of at most 0.0058.
Values may be sent and summed in bfloat16 or wider, within the bound.
A program may use at most 64 MiB of HBM per device.

```python
import math
import jax
import jax.numpy as jnp
from jax import lax

D = 3584
FF = 1024
EXP_NODE = 2
TOPK = 8
TOPN = 4
TOK_NODE = 16
TOKENS = 256
EXPERTS = 32
CAP_N = 8
N_NODE = 16
N_CHIP = 2


def route_block(key):
    key_count, key_node, key_token, key_order = jax.random.split(key, 4)
    pairs = N_NODE // 2
    shares = jax.random.randint(key_count, (pairs,), 0, CAP_N + 1, dtype=jnp.int32)
    shares = shares.at[0].set(CAP_N)
    counts = jnp.stack([shares, CAP_N - shares], axis=1).reshape(N_NODE)
    ends = jnp.cumsum(counts).astype(jnp.int32)
    starts = ends - counts
    entry = jnp.arange(TOPN * TOK_NODE, dtype=jnp.int32)
    group = jnp.sum((entry[:, None] >= ends[None, :]).astype(jnp.int32), axis=1)
    slot = entry - starts[group]
    token = entry % TOK_NODE
    column = entry // TOK_NODE
    labels = jax.random.permutation(key_node, N_NODE).astype(jnp.int32)
    node = labels[group]
    token_perm = jax.random.permutation(key_token, TOK_NODE).astype(jnp.int32)
    owner = token_perm[token]
    node_grid = jnp.zeros((TOK_NODE, TOPN), jnp.int32).at[owner, column].set(node)
    slot_grid = jnp.zeros((TOK_NODE, TOPN), jnp.int32).at[owner, column].set(slot)
    local = jnp.arange(EXP_NODE, dtype=jnp.int32)
    ids_full = (node_grid[:, :, None] * EXP_NODE + local[None, None, :]).reshape(TOK_NODE, TOPK)
    slots_full = jnp.broadcast_to(slot_grid[:, :, None], (TOK_NODE, TOPN, EXP_NODE)).reshape(TOK_NODE, TOPK)
    scores = jax.random.randint(key_order, (TOK_NODE, TOPK), 0, 1 << 20, dtype=jnp.int32) * TOPK + jnp.arange(TOPK, dtype=jnp.int32)[None, :]
    order = jnp.argsort(scores, axis=1, stable=True).astype(jnp.int32)
    return (jnp.take_along_axis(ids_full, order, axis=1), jnp.take_along_axis(slots_full, order, axis=1))


def route_all(key):
    base = jax.random.fold_in(key, 7331)
    node_keys = jax.vmap(lambda index: jax.random.fold_in(base, index))(jnp.arange(N_NODE, dtype=jnp.int32))
    ids_all, slots_all = jax.vmap(route_block)(node_keys)
    return (ids_all.reshape(TOKENS, TOPK), slots_all.reshape(TOKENS, TOPK))


def draw_expert_ids(key, part):
    return route_all(key)[0]


def draw_slot_ids(key, part):
    return route_all(key)[1]


def block_scale(key, extent, shards, low, high):
    factor_of = 1.0
    for dim, parts in shards:
        heights = jax.random.uniform(jax.random.fold_in(jax.random.fold_in(key, 6), dim), (parts,), jnp.float32, low / len(shards), high / len(shards))
        factor_of = factor_of * jnp.repeat(jnp.exp(heights), extent[dim] // parts).reshape((-1,) + (1,) * (len(extent) - 1 - dim))
    return factor_of


def noise(stream_key, dims, width, bound, pieces=(), held_as=jnp.bfloat16):
    level = block_scale(stream_key, dims, pieces, -0.22, 0.18) if pieces else 1.0
    values = jax.random.normal(stream_key, dims, jnp.float32) * width * level
    return jnp.minimum(jnp.maximum(values, -bound), bound).astype(held_as)


def setup_inputs(seed: int = 0) -> dict:
    key_of = jax.random.split(jax.random.key(seed), 7)
    return {
        "tokens": noise(key_of[0], (TOKENS, D), 1.0, 6.0, ((0, 32),)),
        "expert_ids": draw_expert_ids(jax.random.fold_in(key_of[6], 71), 0),
        "gate_values": jnp.clip(jnp.exp(math.log(1.0) - 2.306499 * jax.random.uniform(key_of[2], (TOKENS, TOPK), jnp.float32) ** block_scale(key_of[2], (TOKENS, TOPK), ((0, 32),), -0.2, 0.2)), 0.099609375, 1.0).astype(jnp.bfloat16),
        "slot_ids": draw_slot_ids(jax.random.fold_in(key_of[6], 71), 0),
        "up_weight": noise(key_of[4], (EXPERTS, D, FF), D ** -0.5, 0.09375, ((0, 16), (2, 2))),
        "down_weight": noise(key_of[5], (EXPERTS, FF, D), FF ** -0.5, 0.1875, ((0, 16), (1, 2))),
    }


def reference(tokens, expert_ids, gate_values, slot_ids, up_weight, down_weight):
    rows_node = N_NODE * CAP_N
    block_width = FF // N_CHIP
    token_index = jnp.arange(TOKENS, dtype=jnp.int32)
    source_node = token_index // TOK_NODE
    flat_rows = (expert_ids // EXP_NODE) * rows_node + source_node[:, None] * CAP_N + slot_ids
    flat_rows = flat_rows.astype(jnp.int32).reshape(-1)
    owner_ids = jnp.broadcast_to(token_index[:, None], expert_ids.shape).reshape(-1)
    owners = jnp.full((N_NODE * rows_node,), TOKENS, jnp.int32).at[flat_rows].set(owner_ids)
    local_ids = (expert_ids % EXP_NODE).astype(jnp.int32).reshape(-1)
    gate_table = jnp.zeros((N_NODE * rows_node, EXP_NODE), jnp.float32)
    gate_table = gate_table.at[flat_rows, local_ids].set(gate_values.astype(jnp.float32).reshape(-1))
    padded = jnp.concatenate([tokens, jnp.zeros((1, D), tokens.dtype)], axis=0)
    owners = owners.reshape(N_NODE, rows_node)
    gate_table = gate_table.reshape(N_NODE, rows_node, EXP_NODE)
    up_nodes = up_weight.reshape(N_NODE, EXP_NODE, D, FF)
    down_nodes = down_weight.reshape(N_NODE, EXP_NODE, FF, D)

    def serve(totals, inputs):
        node_owners, node_gates, up_node, down_node = inputs
        routed = padded[node_owners]
        result = jnp.zeros((rows_node, N_CHIP, D), jnp.float32)
        for expert in range(EXP_NODE):
            hidden = jax.nn.silu(jnp.dot(routed, up_node[expert], preferred_element_type=jnp.float32)).astype(jnp.bfloat16)
            blocks = hidden.reshape(rows_node, N_CHIP, block_width).astype(jnp.float32)
            down_blocks = down_node[expert].reshape(N_CHIP, block_width, D).astype(jnp.float32)
            result = result + node_gates[:, expert][:, None, None] * jnp.einsum("rcf,cfd->rcd", blocks, down_blocks)
        rounded = lax.optimization_barrier(result.astype(jnp.bfloat16))
        served = jnp.sum(rounded.astype(jnp.float32), axis=1)
        return totals.at[node_owners].add(served), None

    totals = jnp.zeros((TOKENS + 1, D), jnp.float32)
    totals, unused = lax.scan(serve, totals, (owners, gate_table, up_nodes, down_nodes))
    return totals[:TOKENS].astype(jnp.bfloat16)
```

```python
import functools

import jax
import jax.numpy as jnp
from jax import lax
from jax.experimental import pallas as pl
from jax.experimental.pallas import tpu as pltpu
from jax.sharding import PartitionSpec as P


def pack_rows(targets, experts, node_tokens, node_gates, row_count, per_node):
    row_ids = jnp.arange(row_count, dtype=jnp.int32)
    matches = (targets[None, :, :] == row_ids[:, None, None]).astype(jnp.bfloat16)
    picked = jnp.minimum(jnp.sum(matches.astype(jnp.float32), axis=2), 1.0).astype(jnp.bfloat16)
    packed = jnp.dot(picked, node_tokens, preferred_element_type=jnp.float32).astype(jnp.bfloat16)
    choose = (experts[:, :, None] == jnp.arange(per_node, dtype=jnp.int32)[None, None, :]).astype(
        jnp.bfloat16
    )
    weighted = choose * node_gates[:, :, None]
    gate_rows = jnp.einsum(
        "rtk,tke->re", matches, weighted, preferred_element_type=jnp.float32
    ).astype(jnp.bfloat16)
    return (packed, gate_rows)


def expert_rows(row_block, gate_block, up_local, down_local):
    result = jnp.zeros((row_block.shape[0], down_local.shape[2]), jnp.float32)
    for expert in range(up_local.shape[0]):
        hidden = jax.nn.silu(
            jnp.dot(row_block, up_local[expert], preferred_element_type=jnp.float32)
        ).astype(jnp.bfloat16)
        product = jnp.dot(hidden, down_local[expert], preferred_element_type=jnp.float32)
        result = result + gate_block[:, expert : expert + 1].astype(jnp.float32) * product
    return result.astype(jnp.bfloat16)


def gather_sum(indices, table):
    valid = indices >= 0
    safe = jnp.where(valid, indices, 0).reshape(-1)
    picked = jnp.take(table, safe, axis=0).reshape(
        indices.shape[0], indices.shape[1], table.shape[1]
    )
    return jnp.sum(jnp.where(valid[:, :, None], picked, 0.0), axis=1)


def shards(tokens, expert_ids, gate_values, slot_ids, up_weight, down_weight):
    node_count = lax.axis_size("node")
    chip_count = lax.axis_size("chip")
    my_chip = lax.axis_index("chip")
    tok_dev = tokens.shape[0]
    model_dim = tokens.shape[1]
    per_node = up_weight.shape[0]
    capacity = 8 * chip_count * tok_dev // node_count
    block_cap = capacity // chip_count
    route_code = (expert_ids // per_node * capacity + slot_ids) * per_node + expert_ids % per_node
    node_tokens, node_gates = (
        lax.all_gather(tokens, "chip", axis=0, tiled=True),
        lax.all_gather(gate_values, "chip", axis=0, tiled=True),
    )
    node_codes = lax.all_gather(route_code, "chip", axis=0, tiled=True)
    node_expert = node_codes % per_node
    node_slot = node_codes // per_node % capacity
    node_dest = node_codes // per_node // capacity
    targets = node_dest * capacity + node_slot
    packed, gate_rows = pack_rows(
        targets, node_expert, node_tokens, node_gates, node_count * capacity, per_node
    )
    shaped = packed.reshape(node_count, chip_count, 1, block_cap, model_dim)
    gate_shaped = gate_rows.reshape(node_count, chip_count, 1, block_cap, per_node)
    arrived, arrived_gates = (
        lax.all_to_all(shaped, "node", split_axis=0, concat_axis=2, tiled=True),
        lax.all_to_all(gate_shaped, "node", split_axis=0, concat_axis=2, tiled=True),
    )
    row_block = arrived.reshape(-1, model_dim)
    gate_block = arrived_gates.reshape(-1, per_node)
    partial_value = expert_rows(row_block, gate_block, up_weight, down_weight)
    pieces = lax.all_to_all(
        partial_value.reshape(chip_count, node_count * block_cap, model_dim),
        "chip",
        split_axis=0,
        concat_axis=0,
        tiled=True,
    )
    slot_sums = jnp.sum(pieces.astype(jnp.float32), axis=0).reshape(
        node_count, block_cap, model_dim
    )
    held = lax.all_to_all(slot_sums, "node", split_axis=0, concat_axis=0, tiled=True).reshape(
        node_count * block_cap, model_dim
    )
    wanted = (node_slot // block_cap == my_chip) & (node_expert == 0)
    indices = jnp.where(wanted, node_dest * block_cap + node_slot % block_cap, -1)
    term = gather_sum(indices, held)
    summed = lax.psum_scatter(term, "chip", scatter_dimension=0, tiled=True)
    return summed.astype(jnp.bfloat16)


LANES = 128
MESH = pl.DeviceIdType.MESH
TILES = (6, 8, 8, 6)
PIECES = (7, 6, 8, 7)


def fused_kernel(
    tokens_ref, ids_ref, gates_ref, up_hbm, down_hbm, out_ref,
    ids_v, gates_v, up_v, down_v, gath, rows_v, acc, hid_v, total,
    core_out, core_in, one_out, one_in, two_out, two_in, near_out, near_in,
    local_sem, up_sem, down_sem, send_sem, recv_sem,
):
    f32, bf16 = jnp.float32, jnp.bfloat16
    node, x = lax.axis_index("node"), lax.axis_index("chip")
    c = lax.rem(node, 2)
    y = lax.rem(lax.div(node, 2), 2)
    z = lax.div(node, 4)
    nz = 4
    tok, model = tokens_ref.shape
    per_node, _, width = up_v.shape
    group = 4 * nz
    half = group * tok

    def dev(zz, yy, cc, xx):
        return ((zz * 2 + yy) * 2 + cc, xx)

    def block(cc, xx, yy, zz):
        return ((cc * 2 + xx) * 2 + yy) * nz + zz

    z_at = [z, z + 1 - 2 * lax.rem(z, 2), lax.rem(z + 2, nz), nz - 1 - z]
    plane_at = [(x, y), (1 - x, y), (x, 1 - y), (1 - x, 1 - y)]
    z_peer = [dev(zz, y, c, x) for zz in z_at]
    z_other = [dev(zz, y, 1 - c, x) for zz in z_at]
    plane_peer = [dev(z, yy, c, xx) for xx, yy in plane_at]
    plane_other = [dev(z, yy, 1 - c, xx) for xx, yy in plane_at]
    c_peer = z_other[0]

    barrier = pltpu.get_barrier_semaphore()
    peers = z_peer[1:] + plane_peer[1:] + z_other + plane_other[1:]
    for peer in peers:
        pl.semaphore_signal(barrier, inc=1, device_id=peer, device_id_type=MESH)

    own = block(c, x, y, z)
    first = TILES[0] * LANES
    parts, begin = {}, 0
    for name, size in zip(("l1", "l2", "l3", "e"), TILES):
        size = size * LANES + (LANES if name == "l2" else 0)
        parts[name] = pl.ds(begin, size)
        begin += size
    local = [
        pltpu.make_async_copy(ids_ref, ids_v, local_sem.at[0]),
        pltpu.make_async_copy(gates_ref, gates_v, local_sem.at[1]),
        pltpu.make_async_copy(
            tokens_ref.at[:, pl.ds(0, first)], gath.at[own, :, pl.ds(0, first)], local_sem.at[2]
        ),
        pltpu.make_async_copy(
            tokens_ref.at[:, pl.ds(first, model - first)],
            gath.at[own, :, pl.ds(first + LANES, model - first)],
            local_sem.at[3],
        ),
    ]
    for copy in local:
        copy.start()
    up_copies = [
        pltpu.make_async_copy(up_hbm.at[e], up_v.at[e], up_sem.at[e]) for e in range(per_node)
    ]
    down_copies = [
        pltpu.make_async_copy(
            down_hbm.at[e], down_v.at[pl.ds(e * width, width)], down_sem.at[e]
        )
        for e in range(per_node)
    ]

    sends = []

    def send(src, dst, peer):
        copy = pltpu.make_async_remote_copy(
            src_ref=src, dst_ref=dst,
            send_sem=send_sem.at[len(sends)], recv_sem=recv_sem.at[len(sends)],
            device_id=peer, device_id_type=MESH,
        )
        copy.start()
        sends.append(copy)
        return copy

    arriving = {}

    def need(key):
        if key in arriving:
            arriving.pop(key).wait_recv()

    def block_of(g, j):
        return block(c, plane_at[g][0], plane_at[g][1], z_at[j])

    def pass_on(part, source, target, peer):
        ref = gath.at[block_of(*source), :, parts[part]]
        arriving[(part,) + target] = send(ref, ref, peer)

    def own_z(part):
        for j in range(1, nz):
            pass_on(part, (0, 0), (0, j), z_peer[j])

    def own_plane(part, gs=(1, 2, 3)):
        for g in gs:
            pass_on(part, (0, 0), (g, 0), plane_peer[g])

    def z_plane(part, j, gs=(1, 2, 3)):
        need((part, 0, j))
        for g in gs:
            pass_on(part, (0, j), (g, j), plane_peer[g])

    def plane_z(part, g):
        need((part, g, 0))
        for j in range(1, nz):
            pass_on(part, (g, 0), (g, j), z_peer[j])

    def cross(part, j):
        g = 1 + j % 2
        need((part, g, j))
        pass_on(part, (g, j), (3, j), plane_peer[3 - g])

    def gathered(part):
        for g in range(4):
            for j in range(nz):
                need((part, g, j))

    def share(cols):
        ref = gath.at[pl.ds(c * group, group), :, cols]
        return send(ref, ref, c_peer)

    pl.semaphore_wait(barrier, len(peers))
    local[2].wait()
    own_z("l1")
    local[3].wait()
    own_plane("e")
    own_plane("l1")
    local[0].wait()
    local[1].wait()
    table = jnp.zeros((tok, LANES), f32)
    lanes = lax.broadcasted_iota(jnp.int32, (tok, LANES), 1)
    ids = ids_v[...]
    gates = gates_v[...].astype(f32)
    for k in range(ids.shape[1]):
        table = table + jnp.where(ids[:, k : k + 1] == lanes, gates[:, k : k + 1], 0.0)
    gath[own, :, pl.ds(first, LANES)] = table.astype(bf16)
    def weights(side):
        lane = lax.broadcasted_iota(jnp.int32, (half, LANES), 1)
        table = gath[pl.ds(side * group, group), :, pl.ds(first, LANES)]
        table = table.astype(f32).reshape(half, LANES)
        return [
            jnp.sum(jnp.where(lane == node * per_node + e, table, 0.0), axis=1, keepdims=True)
            for e in range(per_node)
        ]

    def project(a, n, sides, weight=None):
        cols = pl.ds(a if a < first else a + LANES, n)
        for side in sides:
            start = (lax.rem(c + side, 2)) * group

            def pack(i, carry):
                pair = gath[pl.ds(start + 2 * i, 2), :, cols].astype(f32)
                row = pl.multiple_of(side * half + 2 * tok * i, 2 * tok)
                rows_v[pl.ds(row, 2 * tok), pl.ds(a, n)] = pair.reshape(2 * tok, n).astype(bf16)
                return carry

            lax.fori_loop(0, group // 2, pack, 0)
        rows = pl.ds(sides[0] * half, len(sides) * half)
        for e in range(per_node):
            value = jnp.dot(
                rows_v[rows, pl.ds(a, n)], up_v[e, pl.ds(a, n)], preferred_element_type=f32
            )
            if a:
                value = value + acc[e, rows]
            if weight is None:
                acc[e, rows] = value
            else:
                value = weight[e] * (value / (1.0 + jnp.exp(-value)))
                hid_v[rows, pl.ds(e * width, width)] = value.astype(bf16)

    n1, n2 = first, TILES[1] * LANES
    n3 = model - n1 - n2
    own_z("l2")
    own_plane("l2")
    own_z("l3")
    own_plane("l3")
    for copy in up_copies + down_copies:
        copy.start()
    z_plane("l1", 1)
    z_plane("l1", 2)
    z_plane("l1", 3)
    plane_z("e", 1)
    plane_z("e", 2)
    z_plane("l2", 1)
    z_plane("l2", 2)
    z_plane("l2", 3)
    plane_z("e", 3)
    z_plane("l3", 1)
    z_plane("l3", 2)
    z_plane("l3", 3)
    own_z("e")

    n1, n2 = first, TILES[1] * LANES
    n3 = model - n1 - n2
    gathered("l1")
    share1 = share(parts["l1"])
    gathered("l2")
    share2 = share(parts["l2"])
    share1.wait_recv()
    for copy in up_copies:
        copy.wait()
    project(0, n1, (0, 1))
    share2.wait_recv()
    project(n1, n2, (0, 1))
    weight = [weights(c), weights(1 - c)]
    gathered("l3")
    gathered("e")
    share3 = share(pl.ds(n1 + n2 + LANES, n3))
    project(n1 + n2, n3, (0,), weight[0])

    count = len(PIECES)
    sizes = [n * LANES for n in PIECES]
    piece_at = [sum(sizes[:q]) for q in range(count)]
    corer, planer, zr = {}, {}, {}

    def span(q):
        return pl.ds(piece_at[q], sizes[q])

    def chips(g):
        return (plane_at[g][0] * 2 + plane_at[g][1]) * nz

    def produce_sent(q):
        value = jnp.dot(hid_v[:half], down_v[:, span(q)], preferred_element_type=f32)
        send_core(q, value)

    def send_core(q, value):
        core_out[:, :, span(q)] = value.reshape(group, tok, sizes[q]).astype(bf16)
        ref = (slice(None), slice(None), span(q))
        corer[q] = send(core_out.at[ref], core_in.at[ref], c_peer)

    def produce_kept(q):
        value = jnp.dot(hid_v[half:], down_v[:, span(q)], preferred_element_type=f32)
        total[:, :, span(q)] = value.reshape(group, tok, sizes[q])

    def produce(q):
        value = jnp.dot(hid_v[...], down_v[:, span(q)], preferred_element_type=f32)
        send_core(q, value[:half])
        total[:, :, span(q)] = value[half:].reshape(group, tok, sizes[q])

    def summed(q, where):
        return total[where, :, span(q)] + core_in[where, :, span(q)].astype(f32)

    def plane_first(q):
        corer[q].wait_recv()
        for g in (3, 1, 2):
            slots = pl.ds((g - 1) * nz, nz)
            one_out[slots, :, span(q)] = summed(q, pl.ds(chips(g), nz)).astype(bf16)
            ref = (slots, slice(None), span(q))
            planer[q, g] = send(one_out.at[ref], one_in.at[ref], plane_peer[g])

    def plane_then_z(q):
        value = summed(q, pl.ds(chips(0), nz))
        for g in (1, 2, 3):
            planer[q, g].wait_recv()
            value = value + one_in[(g - 1) * nz : g * nz, :, span(q)].astype(f32)
        total[pl.ds(chips(0), nz), :, span(q)] = value
        send_z(q)

    def send_z(q):
        for j in range(1, nz):
            two_out[j - 1, :, span(q)] = total[chips(0) + z_at[j], :, span(q)].astype(bf16)
            ref = (j - 1, slice(None), span(q))
            zr[q, j] = send(two_out.at[ref], two_in.at[ref], z_other[j])
        near(q)

    def pair(q, slot):
        return one_in[pl.ds(slot, 2), :, span(q)].astype(f32)

    def at_chips(xx, yy, zz):
        return pl.ds((xx * 2 + yy) * nz + zz, 2)

    def ship(q, slot, length, peer):
        ref = (pl.ds(slot, length), slice(None), span(q))
        planer[q, slot] = send(one_out.at[ref], one_in.at[ref], peer)

    def fold_first(q):
        corer[q].wait_recv()
        for yy in range(2):
            value = summed(q, at_chips(1 - x, yy, 0))
            one_out[pl.ds(2 * yy, 2), :, span(q)] = value.astype(bf16)
        ship(q, 0, 4, plane_peer[1])
        for xx in range(2):
            value = summed(q, at_chips(xx, 1 - y, 2))
            one_out[pl.ds(4 + 2 * xx, 2), :, span(q)] = value.astype(bf16)
        ship(q, 4, 4, plane_peer[2])

    def fold_second(q):
        planer[q, 0].wait_recv()
        value = summed(q, at_chips(x, 1 - y, 0)) + pair(q, 2 * (1 - y))
        one_out[pl.ds(8, 2), :, span(q)] = value.astype(bf16)
        ship(q, 8, 2, plane_peer[2])
        planer[q, 4].wait_recv()
        value = summed(q, at_chips(1 - x, y, 2)) + pair(q, 4 + 2 * (1 - x))
        one_out[pl.ds(10, 2), :, span(q)] = value.astype(bf16)
        ship(q, 10, 2, plane_peer[1])

    def fold_then_z(q):
        planer[q, 8].wait_recv()
        planer[q, 10].wait_recv()
        for zz, slots in ((0, (2 * y, 8)), (2, (4 + 2 * x, 10))):
            where = at_chips(x, y, zz)
            value = summed(q, where)
            for slot in slots:
                value = value + pair(q, slot)
            total[where, :, span(q)] = value
        send_z(q)

    def near(q):
        near_out[:, span(q)] = total[chips(0) + z, :, span(q)]
        ref = (slice(None), span(q))
        zr[q, 0] = send(near_out.at[ref], near_in.at[ref], c_peer)

    def z_first(q):
        corer[q].wait_recv()
        for j in (3, 2, 1):
            for g in range(4):
                slot = (j - 1) * 4 + g
                one_out[slot, :, span(q)] = summed(q, chips(g) + z_at[j]).astype(bf16)
            ref = (pl.ds((j - 1) * 4, 4), slice(None), span(q))
            planer[q, j] = send(one_out.at[ref], one_in.at[ref], z_peer[j])

    def z_then_plane(q):
        for j in range(1, nz):
            planer[q, j].wait_recv()
        for g in range(4):
            value = summed(q, chips(g) + z)
            for j in range(1, nz):
                value = value + one_in[(j - 1) * 4 + g, :, span(q)].astype(f32)
            if g == 0:
                total[chips(0) + z, :, span(q)] = value
            else:
                two_out[g - 1, :, span(q)] = value.astype(bf16)
                ref = (g - 1, slice(None), span(q))
                zr[q, g] = send(two_out.at[ref], two_in.at[ref], plane_other[g])
        near(q)

    def finish(q):
        zr[q, 0].wait_recv()
        value = near_in[:, span(q)]
        for j in range(1, nz):
            zr[q, j].wait_recv()
            value = value + two_in[j - 1, :, span(q)].astype(f32)
        out_ref[:, span(q)] = value.astype(out_ref.dtype)

    for copy in down_copies:
        copy.wait()
    produce_sent(0)
    produce_sent(1)
    share3.wait_recv()
    project(n1 + n2, n3, (1,), weight[1])
    produce_kept(0)
    plane_first(0)
    produce_kept(1)
    z_first(1)
    produce(2)
    produce(3)
    plane_first(2)
    plane_first(3)
    plane_then_z(0)
    z_then_plane(1)
    plane_then_z(2)
    plane_then_z(3)
    finish(0)
    finish(1)
    finish(2)
    finish(3)
    for copy in sends:
        copy.wait_send()


def fused(tokens, expert_ids, gate_values, up_weight, down_weight):
    tok, model = tokens.shape
    per_node, _, width = up_weight.shape
    bf16, f32 = jnp.bfloat16, jnp.float32
    nz = 4
    group = 4 * nz
    vmem = pl.BlockSpec(memory_space=pltpu.VMEM)
    anyspace = pl.BlockSpec(memory_space=pl.ANY)
    dma = pltpu.SemaphoreType.DMA
    copies = 95
    return pl.pallas_call(
        fused_kernel,
        out_shape=pltpu.VMEM((tok, model), bf16),
        in_specs=[anyspace] * 5,
        out_specs=vmem,
        scratch_shapes=[
            pltpu.VMEM(expert_ids.shape, jnp.int32),
            pltpu.VMEM(gate_values.shape, bf16),
            pltpu.VMEM(up_weight.shape, bf16),
            pltpu.VMEM((per_node * width, model), bf16),
            pltpu.VMEM((2 * group, tok, model + LANES), bf16),
            pltpu.VMEM((2 * group * tok, model), bf16),
            pltpu.VMEM((per_node, 2 * group * tok, width), f32),
            pltpu.VMEM((2 * group * tok, per_node * width), bf16),
            pltpu.VMEM((group, tok, model), f32),
            pltpu.VMEM((group, tok, model), bf16),
            pltpu.VMEM((group, tok, model), bf16),
            pltpu.VMEM((3 * nz, tok, model), bf16),
            pltpu.VMEM((3 * nz, tok, model), bf16),
            pltpu.VMEM((3, tok, model), bf16),
            pltpu.VMEM((3, tok, model), bf16),
            pltpu.VMEM((tok, model), f32),
            pltpu.VMEM((tok, model), f32),
            dma((4,)), dma((per_node,)), dma((per_node,)),
            dma((copies,)), dma((copies,)),
        ],
        compiler_params=pltpu.CompilerParams(
            collective_id=0, has_side_effects=True, vmem_limit_bytes=60 * 1024 * 1024
        ),
    )(tokens, expert_ids, gate_values, up_weight, down_weight)


def body_for(mesh):
    nodes, chips = mesh.shape["node"], mesh.shape["chip"]
    nz = nodes // 4

    def body(tokens, expert_ids, gate_values, slot_ids, up_weight, down_weight):
        tok, model = tokens.shape
        experts = nodes * up_weight.shape[0]
        if (
            chips == 2
            and nodes == 4 * nz
            and nz == 4
            and tok == 8
            and model == sum(TILES) * LANES == sum(PIECES) * LANES
            and experts <= LANES
        ):
            return fused(tokens, expert_ids, gate_values, up_weight, down_weight)
        return shards(tokens, expert_ids, gate_values, slot_ids, up_weight, down_weight)

    return body


def solution(mesh):
    return jax.shard_map(
        body_for(mesh),
        mesh=mesh,
        in_specs=(
            P(("node", "chip"), None),
            P(("node", "chip"), None),
            P(("node", "chip"), None),
            P(("node", "chip"), None),
            P("node", None, "chip"),
            P("node", "chip", None),
        ),
        out_specs=P(("node", "chip"), None),
        check_vma=False,
    )
```

```python
import functools

import jax
import jax.numpy as jnp
from jax import lax
from jax.experimental import pallas as pl
from jax.experimental.pallas import tpu as pltpu
from jax.sharding import PartitionSpec as P


def pack_rows(targets, experts, node_tokens, node_gates, row_count, per_node):
    row_ids = jnp.arange(row_count, dtype=jnp.int32)
    matches = (targets[None, :, :] == row_ids[:, None, None]).astype(jnp.bfloat16)
    picked = jnp.minimum(jnp.sum(matches.astype(jnp.float32), axis=2), 1.0).astype(jnp.bfloat16)
    packed = jnp.dot(picked, node_tokens, preferred_element_type=jnp.float32).astype(jnp.bfloat16)
    choose = (experts[:, :, None] == jnp.arange(per_node, dtype=jnp.int32)[None, None, :]).astype(
        jnp.bfloat16
    )
    weighted = choose * node_gates[:, :, None]
    gate_rows = jnp.einsum(
        "rtk,tke->re", matches, weighted, preferred_element_type=jnp.float32
    ).astype(jnp.bfloat16)
    return (packed, gate_rows)


def expert_rows(row_block, gate_block, up_local, down_local):
    result = jnp.zeros((row_block.shape[0], down_local.shape[2]), jnp.float32)
    for expert in range(up_local.shape[0]):
        hidden = jax.nn.silu(
            jnp.dot(row_block, up_local[expert], preferred_element_type=jnp.float32)
        ).astype(jnp.bfloat16)
        product = jnp.dot(hidden, down_local[expert], preferred_element_type=jnp.float32)
        result = result + gate_block[:, expert : expert + 1].astype(jnp.float32) * product
    return result.astype(jnp.bfloat16)


def gather_sum(indices, table):
    valid = indices >= 0
    safe = jnp.where(valid, indices, 0).reshape(-1)
    picked = jnp.take(table, safe, axis=0).reshape(
        indices.shape[0], indices.shape[1], table.shape[1]
    )
    return jnp.sum(jnp.where(valid[:, :, None], picked, 0.0), axis=1)


def shards(tokens, expert_ids, gate_values, slot_ids, up_weight, down_weight):
    node_count = lax.axis_size("node")
    chip_count = lax.axis_size("chip")
    my_chip = lax.axis_index("chip")
    tok_dev = tokens.shape[0]
    model_dim = tokens.shape[1]
    per_node = up_weight.shape[0]
    capacity = 8 * chip_count * tok_dev // node_count
    block_cap = capacity // chip_count
    route_code = (expert_ids // per_node * capacity + slot_ids) * per_node + expert_ids % per_node
    node_tokens, node_gates = (
        lax.all_gather(tokens, "chip", axis=0, tiled=True),
        lax.all_gather(gate_values, "chip", axis=0, tiled=True),
    )
    node_codes = lax.all_gather(route_code, "chip", axis=0, tiled=True)
    node_expert = node_codes % per_node
    node_slot = node_codes // per_node % capacity
    node_dest = node_codes // per_node // capacity
    targets = node_dest * capacity + node_slot
    packed, gate_rows = pack_rows(
        targets, node_expert, node_tokens, node_gates, node_count * capacity, per_node
    )
    shaped = packed.reshape(node_count, chip_count, 1, block_cap, model_dim)
    gate_shaped = gate_rows.reshape(node_count, chip_count, 1, block_cap, per_node)
    arrived, arrived_gates = (
        lax.all_to_all(shaped, "node", split_axis=0, concat_axis=2, tiled=True),
        lax.all_to_all(gate_shaped, "node", split_axis=0, concat_axis=2, tiled=True),
    )
    row_block = arrived.reshape(-1, model_dim)
    gate_block = arrived_gates.reshape(-1, per_node)
    partial_value = expert_rows(row_block, gate_block, up_weight, down_weight)
    pieces = lax.all_to_all(
        partial_value.reshape(chip_count, node_count * block_cap, model_dim),
        "chip",
        split_axis=0,
        concat_axis=0,
        tiled=True,
    )
    slot_sums = jnp.sum(pieces.astype(jnp.float32), axis=0).reshape(
        node_count, block_cap, model_dim
    )
    held = lax.all_to_all(slot_sums, "node", split_axis=0, concat_axis=0, tiled=True).reshape(
        node_count * block_cap, model_dim
    )
    wanted = (node_slot // block_cap == my_chip) & (node_expert == 0)
    indices = jnp.where(wanted, node_dest * block_cap + node_slot % block_cap, -1)
    term = gather_sum(indices, held)
    summed = lax.psum_scatter(term, "chip", scatter_dimension=0, tiled=True)
    return summed.astype(jnp.bfloat16)


LANES = 128
MESH = pl.DeviceIdType.MESH
TILES = (5, 7, 9, 7)
PIECES = (7, 6, 8, 4, 3)


def fused_kernel(
    tokens_ref, ids_ref, gates_ref, up_hbm, down_hbm, out_ref,
    ids_v, gates_v, up_v, down_v, gath, rows_v, acc, hid_v, total,
    core_out, core_in, one_out, one_in, two_out, two_in, near_out, near_in,
    local_sem, up_sem, down_sem, send_sem, recv_sem,
):
    f32, bf16 = jnp.float32, jnp.bfloat16
    node, x = lax.axis_index("node"), lax.axis_index("chip")
    c = lax.rem(node, 2)
    y = lax.rem(lax.div(node, 2), 2)
    z = lax.div(node, 4)
    nz = 4
    tok, model = tokens_ref.shape
    per_node, _, width = up_v.shape
    group = 4 * nz
    half = group * tok

    def dev(zz, yy, cc, xx):
        return ((zz * 2 + yy) * 2 + cc, xx)

    def block(cc, xx, yy, zz):
        return ((cc * 2 + xx) * 2 + yy) * nz + zz

    z_at = [z, z + 1 - 2 * lax.rem(z, 2), lax.rem(z + 2, nz), nz - 1 - z]
    plane_at = [(x, y), (1 - x, y), (x, 1 - y), (1 - x, 1 - y)]
    z_peer = [dev(zz, y, c, x) for zz in z_at]
    z_other = [dev(zz, y, 1 - c, x) for zz in z_at]
    plane_peer = [dev(z, yy, c, xx) for xx, yy in plane_at]
    plane_other = [dev(z, yy, 1 - c, xx) for xx, yy in plane_at]
    c_peer = z_other[0]

    barrier = pltpu.get_barrier_semaphore()
    peers = z_peer[1:] + plane_peer[1:] + z_other + plane_other[1:]
    for peer in peers:
        pl.semaphore_signal(barrier, inc=1, device_id=peer, device_id_type=MESH)

    own = block(c, x, y, z)
    first = TILES[0] * LANES
    parts, begin = {}, 0
    for name, size in zip(("l1", "l2", "l3", "e"), TILES):
        size = size * LANES + (LANES if name == "l2" else 0)
        parts[name] = pl.ds(begin, size)
        begin += size
    local = [
        pltpu.make_async_copy(ids_ref, ids_v, local_sem.at[0]),
        pltpu.make_async_copy(gates_ref, gates_v, local_sem.at[1]),
        pltpu.make_async_copy(
            tokens_ref.at[:, pl.ds(0, first)], gath.at[own, :, pl.ds(0, first)], local_sem.at[2]
        ),
        pltpu.make_async_copy(
            tokens_ref.at[:, pl.ds(first, model - first)],
            gath.at[own, :, pl.ds(first + LANES, model - first)],
            local_sem.at[3],
        ),
    ]
    for copy in local:
        copy.start()
    up_copies = [
        pltpu.make_async_copy(up_hbm.at[e], up_v.at[e], up_sem.at[e]) for e in range(per_node)
    ]
    down_copies = [
        pltpu.make_async_copy(
            down_hbm.at[e], down_v.at[pl.ds(e * width, width)], down_sem.at[e]
        )
        for e in range(per_node)
    ]

    sends = []

    def send(src, dst, peer):
        copy = pltpu.make_async_remote_copy(
            src_ref=src, dst_ref=dst,
            send_sem=send_sem.at[len(sends)], recv_sem=recv_sem.at[len(sends)],
            device_id=peer, device_id_type=MESH,
        )
        copy.start()
        sends.append(copy)
        return copy

    settled = []

    def settle(count):
        for copy in sends[len(settled) : count]:
            copy.wait_send()
            settled.append(copy)

    arriving = {}

    def need(key):
        if key in arriving:
            arriving.pop(key).wait_recv()

    def block_of(g, j):
        return block(c, plane_at[g][0], plane_at[g][1], z_at[j])

    def pass_on(part, source, target, peer):
        ref = gath.at[block_of(*source), :, parts[part]]
        arriving[(part,) + target] = send(ref, ref, peer)

    def own_z(part):
        for j in range(1, nz):
            pass_on(part, (0, 0), (0, j), z_peer[j])

    def own_plane(part, gs=(1, 2, 3)):
        for g in gs:
            pass_on(part, (0, 0), (g, 0), plane_peer[g])

    def z_plane(part, j, gs=(1, 2, 3)):
        need((part, 0, j))
        for g in gs:
            pass_on(part, (0, j), (g, j), plane_peer[g])

    def plane_z(part, g):
        need((part, g, 0))
        for j in range(1, nz):
            pass_on(part, (g, 0), (g, j), z_peer[j])

    def cross(part, j):
        g = 1 + j % 2
        need((part, g, j))
        pass_on(part, (g, j), (3, j), plane_peer[3 - g])

    def gathered(part):
        for g in range(4):
            for j in range(nz):
                need((part, g, j))

    def share(cols):
        ref = gath.at[pl.ds(c * group, group), :, cols]
        return send(ref, ref, c_peer)

    pl.semaphore_wait(barrier, len(peers))
    local[2].wait()
    own_z("l1")
    local[3].wait()
    own_plane("e")
    own_plane("l1")
    local[0].wait()
    local[1].wait()
    table = jnp.zeros((tok, LANES), f32)
    lanes = lax.broadcasted_iota(jnp.int32, (tok, LANES), 1)
    ids = ids_v[...]
    gates = gates_v[...].astype(f32)
    for k in range(ids.shape[1]):
        table = table + jnp.where(ids[:, k : k + 1] == lanes, gates[:, k : k + 1], 0.0)
    gath[own, :, pl.ds(first, LANES)] = table.astype(bf16)
    def weights(side):
        lane = lax.broadcasted_iota(jnp.int32, (half, LANES), 1)
        table = gath[pl.ds(side * group, group), :, pl.ds(first, LANES)]
        table = table.astype(f32).reshape(half, LANES)
        return [
            jnp.sum(jnp.where(lane == node * per_node + e, table, 0.0), axis=1, keepdims=True)
            for e in range(per_node)
        ]

    def project(a, n, sides, weight=None):
        cols = pl.ds(a if a < first else a + LANES, n)
        for side in sides:
            start = (lax.rem(c + side, 2)) * group

            def pack(i, carry):
                pair = gath[pl.ds(start + 2 * i, 2), :, cols].astype(f32)
                row = pl.multiple_of(side * half + 2 * tok * i, 2 * tok)
                rows_v[pl.ds(row, 2 * tok), pl.ds(a, n)] = pair.reshape(2 * tok, n).astype(bf16)
                return carry

            lax.fori_loop(0, group // 2, pack, 0)
        rows = pl.ds(sides[0] * half, len(sides) * half)
        for e in range(per_node):
            value = jnp.dot(
                rows_v[rows, pl.ds(a, n)], up_v[e, pl.ds(a, n)], preferred_element_type=f32
            )
            if a:
                value = value + acc[e, rows]
            if weight is None:
                acc[e, rows] = value
            else:
                value = (value / (1.0 + jnp.exp(-value))).astype(bf16).astype(f32) * weight[e]
                hid_v[rows, pl.ds(e * width, width)] = value.astype(bf16)

    n1, n2 = first, TILES[1] * LANES
    n3 = model - n1 - n2
    own_z("l2")
    own_plane("l2")
    own_z("l3")
    own_plane("l3")
    for copy in up_copies + down_copies:
        copy.start()
    z_plane("l1", 1)
    z_plane("l1", 2)
    z_plane("l1", 3)
    plane_z("e", 1)
    plane_z("e", 2)
    z_plane("l2", 1)
    z_plane("l2", 2)
    z_plane("l2", 3)
    plane_z("e", 3)
    z_plane("l3", 1)
    z_plane("l3", 2)
    z_plane("l3", 3)
    own_z("e")

    n1, n2 = first, TILES[1] * LANES
    n3 = model - n1 - n2
    gathered("l1")
    share1 = share(parts["l1"])
    gathered("l2")
    share2 = share(parts["l2"])
    share1.wait_recv()
    for copy in up_copies:
        copy.wait()
    project(0, n1, (0, 1))
    share2.wait_recv()
    project(n1, n2, (0, 1))
    weight = [weights(c), weights(1 - c)]
    gathered("l3")
    gathered("e")
    share3 = share(pl.ds(n1 + n2 + LANES, n3))
    project(n1 + n2, n3, (0,), weight[0])

    count = len(PIECES)
    sizes = [n * LANES for n in PIECES]
    piece_at = [sum(sizes[:q]) for q in range(count)]
    corer, planer, zr = {}, {}, {}

    def span(q):
        return pl.ds(piece_at[q], sizes[q])

    def chips(g):
        return (plane_at[g][0] * 2 + plane_at[g][1]) * nz

    def produce_sent(q):
        value = jnp.dot(hid_v[:half], down_v[:, span(q)], preferred_element_type=f32)
        send_core(q, value)

    def send_core(q, value):
        core_out[:, :, span(q)] = value.reshape(group, tok, sizes[q]).astype(bf16)
        ref = (slice(None), slice(None), span(q))
        corer[q] = send(core_out.at[ref], core_in.at[ref], c_peer)

    def produce_kept(q):
        value = jnp.dot(hid_v[half:], down_v[:, span(q)], preferred_element_type=f32)
        total[:, :, span(q)] = value.reshape(group, tok, sizes[q])

    def produce(q):
        value = jnp.dot(hid_v[...], down_v[:, span(q)], preferred_element_type=f32)
        send_core(q, value[:half])
        total[:, :, span(q)] = value[half:].reshape(group, tok, sizes[q])

    def summed(q, where):
        return total[where, :, span(q)] + core_in[where, :, span(q)].astype(f32)

    def plane_first(q):
        corer[q].wait_recv()
        for g in (3, 1, 2):
            slots = pl.ds((g - 1) * nz, nz)
            one_out[slots, :, span(q)] = summed(q, pl.ds(chips(g), nz)).astype(bf16)
            ref = (slots, slice(None), span(q))
            planer[q, g] = send(one_out.at[ref], one_in.at[ref], plane_peer[g])

    def plane_then_z(q):
        value = summed(q, pl.ds(chips(0), nz))
        for g in (1, 2, 3):
            planer[q, g].wait_recv()
            value = value + one_in[(g - 1) * nz : g * nz, :, span(q)].astype(f32)
        total[pl.ds(chips(0), nz), :, span(q)] = value
        send_z(q)

    def send_z(q):
        for j in range(1, nz):
            two_out[j - 1, :, span(q)] = total[chips(0) + z_at[j], :, span(q)].astype(bf16)
            ref = (j - 1, slice(None), span(q))
            zr[q, j] = send(two_out.at[ref], two_in.at[ref], z_other[j])
        near(q)

    def pair(q, slot):
        return one_in[pl.ds(slot, 2), :, span(q)].astype(f32)

    def at_chips(xx, yy, zz):
        return pl.ds((xx * 2 + yy) * nz + zz, 2)

    def ship(q, slot, length, peer):
        ref = (pl.ds(slot, length), slice(None), span(q))
        planer[q, slot] = send(one_out.at[ref], one_in.at[ref], peer)

    def fold_first(q):
        corer[q].wait_recv()
        for yy in range(2):
            value = summed(q, at_chips(1 - x, yy, 0))
            one_out[pl.ds(2 * yy, 2), :, span(q)] = value.astype(bf16)
        ship(q, 0, 4, plane_peer[1])
        for xx in range(2):
            value = summed(q, at_chips(xx, 1 - y, 2))
            one_out[pl.ds(4 + 2 * xx, 2), :, span(q)] = value.astype(bf16)
        ship(q, 4, 4, plane_peer[2])

    def fold_second(q):
        planer[q, 0].wait_recv()
        value = summed(q, at_chips(x, 1 - y, 0)) + pair(q, 2 * (1 - y))
        one_out[pl.ds(8, 2), :, span(q)] = value.astype(bf16)
        ship(q, 8, 2, plane_peer[2])
        planer[q, 4].wait_recv()
        value = summed(q, at_chips(1 - x, y, 2)) + pair(q, 4 + 2 * (1 - x))
        one_out[pl.ds(10, 2), :, span(q)] = value.astype(bf16)
        ship(q, 10, 2, plane_peer[1])

    def fold_then_z(q):
        planer[q, 8].wait_recv()
        planer[q, 10].wait_recv()
        for zz, slots in ((0, (2 * y, 8)), (2, (4 + 2 * x, 10))):
            where = at_chips(x, y, zz)
            value = summed(q, where)
            for slot in slots:
                value = value + pair(q, slot)
            total[where, :, span(q)] = value
        send_z(q)

    def near(q):
        near_out[:, span(q)] = total[chips(0) + z, :, span(q)]
        ref = (slice(None), span(q))
        zr[q, 0] = send(near_out.at[ref], near_in.at[ref], c_peer)

    def z_first(q):
        corer[q].wait_recv()
        for j in (3, 2, 1):
            for g in range(4):
                slot = (j - 1) * 4 + g
                one_out[slot, :, span(q)] = summed(q, chips(g) + z_at[j]).astype(bf16)
            ref = (pl.ds((j - 1) * 4, 4), slice(None), span(q))
            planer[q, j] = send(one_out.at[ref], one_in.at[ref], z_peer[j])

    def z_then_plane(q):
        for j in range(1, nz):
            planer[q, j].wait_recv()
        for g in range(4):
            value = summed(q, chips(g) + z)
            for j in range(1, nz):
                value = value + one_in[(j - 1) * 4 + g, :, span(q)].astype(f32)
            if g == 0:
                total[chips(0) + z, :, span(q)] = value
            else:
                two_out[g - 1, :, span(q)] = value.astype(bf16)
                ref = (g - 1, slice(None), span(q))
                zr[q, g] = send(two_out.at[ref], two_in.at[ref], plane_other[g])
        near(q)

    def finish(q):
        zr[q, 0].wait_recv()
        value = near_in[:, span(q)]
        for j in range(1, nz):
            zr[q, j].wait_recv()
            value = value + two_in[j - 1, :, span(q)].astype(f32)
        out_ref[:, span(q)] = value.astype(out_ref.dtype)

    for copy in down_copies:
        copy.wait()
    gather_count = len(sends)
    produce_sent(0)
    produce_sent(1)
    share3.wait_recv()
    project(n1 + n2, n3, (1,), weight[1])
    produce_kept(0)
    plane_first(0)
    produce_kept(1)
    z_first(1)
    produce(2)
    produce(3)
    plane_first(2)
    produce(4)
    plane_first(3)
    plane_first(4)
    settle(gather_count)
    plane_then_z(0)
    z_then_plane(1)
    plane_then_z(2)
    plane_then_z(3)
    plane_then_z(4)
    finish(0)
    finish(1)
    finish(2)
    finish(3)
    finish(4)
    settle(len(sends))


def fused(tokens, expert_ids, gate_values, up_weight, down_weight):
    tok, model = tokens.shape
    per_node, _, width = up_weight.shape
    bf16, f32 = jnp.bfloat16, jnp.float32
    nz = 4
    group = 4 * nz
    vmem = pl.BlockSpec(memory_space=pltpu.VMEM)
    anyspace = pl.BlockSpec(memory_space=pl.ANY)
    dma = pltpu.SemaphoreType.DMA
    copies = 103
    return pl.pallas_call(
        fused_kernel,
        out_shape=pltpu.VMEM((tok, model), bf16),
        in_specs=[anyspace] * 5,
        out_specs=vmem,
        scratch_shapes=[
            pltpu.VMEM(expert_ids.shape, jnp.int32),
            pltpu.VMEM(gate_values.shape, bf16),
            pltpu.VMEM(up_weight.shape, bf16),
            pltpu.VMEM((per_node * width, model), bf16),
            pltpu.VMEM((2 * group, tok, model + LANES), bf16),
            pltpu.VMEM((2 * group * tok, model), bf16),
            pltpu.VMEM((per_node, 2 * group * tok, width), f32),
            pltpu.VMEM((2 * group * tok, per_node * width), bf16),
            pltpu.VMEM((group, tok, model), f32),
            pltpu.VMEM((group, tok, model), bf16),
            pltpu.VMEM((group, tok, model), bf16),
            pltpu.VMEM((3 * nz, tok, model), bf16),
            pltpu.VMEM((3 * nz, tok, model), bf16),
            pltpu.VMEM((3, tok, model), bf16),
            pltpu.VMEM((3, tok, model), bf16),
            pltpu.VMEM((tok, model), f32),
            pltpu.VMEM((tok, model), f32),
            dma((4,)), dma((per_node,)), dma((per_node,)),
            dma((copies,)), dma((copies,)),
        ],
        compiler_params=pltpu.CompilerParams(
            collective_id=0, has_side_effects=True, vmem_limit_bytes=60 * 1024 * 1024
        ),
    )(tokens, expert_ids, gate_values, up_weight, down_weight)


def body_for(mesh):
    nodes, chips = mesh.shape["node"], mesh.shape["chip"]
    nz = nodes // 4

    def body(tokens, expert_ids, gate_values, slot_ids, up_weight, down_weight):
        tok, model = tokens.shape
        experts = nodes * up_weight.shape[0]
        if (
            chips == 2
            and nodes == 4 * nz
            and nz == 4
            and tok == 8
            and model == sum(TILES) * LANES == sum(PIECES) * LANES
            and experts <= LANES
        ):
            return fused(tokens, expert_ids, gate_values, up_weight, down_weight)
        return shards(tokens, expert_ids, gate_values, slot_ids, up_weight, down_weight)

    return body


def solution(mesh):
    return jax.shard_map(
        body_for(mesh),
        mesh=mesh,
        in_specs=(
            P(("node", "chip"), None),
            P(("node", "chip"), None),
            P(("node", "chip"), None),
            P(("node", "chip"), None),
            P("node", None, "chip"),
            P("node", "chip", None),
        ),
        out_specs=P(("node", "chip"), None),
        check_vma=False,
    )
```

```python
import functools

import jax
import jax.numpy as jnp
from jax import lax
from jax.experimental import pallas as pl
from jax.experimental.pallas import tpu as pltpu
from jax.sharding import PartitionSpec as P


def pack_rows(targets, experts, node_tokens, node_gates, row_count, per_node):
    row_ids = jnp.arange(row_count, dtype=jnp.int32)
    matches = (targets[None, :, :] == row_ids[:, None, None]).astype(jnp.bfloat16)
    picked = jnp.minimum(jnp.sum(matches.astype(jnp.float32), axis=2), 1.0).astype(jnp.bfloat16)
    packed = jnp.dot(picked, node_tokens, preferred_element_type=jnp.float32).astype(jnp.bfloat16)
    choose = (experts[:, :, None] == jnp.arange(per_node, dtype=jnp.int32)[None, None, :]).astype(
        jnp.bfloat16
    )
    weighted = choose * node_gates[:, :, None]
    gate_rows = jnp.einsum(
        "rtk,tke->re", matches, weighted, preferred_element_type=jnp.float32
    ).astype(jnp.bfloat16)
    return (packed, gate_rows)


def expert_rows(row_block, gate_block, up_local, down_local):
    result = jnp.zeros((row_block.shape[0], down_local.shape[2]), jnp.float32)
    for expert in range(up_local.shape[0]):
        hidden = jax.nn.silu(
            jnp.dot(row_block, up_local[expert], preferred_element_type=jnp.float32)
        ).astype(jnp.bfloat16)
        product = jnp.dot(hidden, down_local[expert], preferred_element_type=jnp.float32)
        result = result + gate_block[:, expert : expert + 1].astype(jnp.float32) * product
    return result.astype(jnp.bfloat16)


def gather_sum(indices, table):
    valid = indices >= 0
    safe = jnp.where(valid, indices, 0).reshape(-1)
    picked = jnp.take(table, safe, axis=0).reshape(
        indices.shape[0], indices.shape[1], table.shape[1]
    )
    return jnp.sum(jnp.where(valid[:, :, None], picked, 0.0), axis=1)


def shards(tokens, expert_ids, gate_values, slot_ids, up_weight, down_weight):
    node_count = lax.axis_size("node")
    chip_count = lax.axis_size("chip")
    my_chip = lax.axis_index("chip")
    tok_dev = tokens.shape[0]
    model_dim = tokens.shape[1]
    per_node = up_weight.shape[0]
    capacity = 8 * chip_count * tok_dev // node_count
    block_cap = capacity // chip_count
    route_code = (expert_ids // per_node * capacity + slot_ids) * per_node + expert_ids % per_node
    node_tokens, node_gates = (
        lax.all_gather(tokens, "chip", axis=0, tiled=True),
        lax.all_gather(gate_values, "chip", axis=0, tiled=True),
    )
    node_codes = lax.all_gather(route_code, "chip", axis=0, tiled=True)
    node_expert = node_codes % per_node
    node_slot = node_codes // per_node % capacity
    node_dest = node_codes // per_node // capacity
    targets = node_dest * capacity + node_slot
    packed, gate_rows = pack_rows(
        targets, node_expert, node_tokens, node_gates, node_count * capacity, per_node
    )
    shaped = packed.reshape(node_count, chip_count, 1, block_cap, model_dim)
    gate_shaped = gate_rows.reshape(node_count, chip_count, 1, block_cap, per_node)
    arrived, arrived_gates = (
        lax.all_to_all(shaped, "node", split_axis=0, concat_axis=2, tiled=True),
        lax.all_to_all(gate_shaped, "node", split_axis=0, concat_axis=2, tiled=True),
    )
    row_block = arrived.reshape(-1, model_dim)
    gate_block = arrived_gates.reshape(-1, per_node)
    partial_value = expert_rows(row_block, gate_block, up_weight, down_weight)
    pieces = lax.all_to_all(
        partial_value.reshape(chip_count, node_count * block_cap, model_dim),
        "chip",
        split_axis=0,
        concat_axis=0,
        tiled=True,
    )
    slot_sums = jnp.sum(pieces.astype(jnp.float32), axis=0).reshape(
        node_count, block_cap, model_dim
    )
    held = lax.all_to_all(slot_sums, "node", split_axis=0, concat_axis=0, tiled=True).reshape(
        node_count * block_cap, model_dim
    )
    wanted = (node_slot // block_cap == my_chip) & (node_expert == 0)
    indices = jnp.where(wanted, node_dest * block_cap + node_slot % block_cap, -1)
    term = gather_sum(indices, held)
    summed = lax.psum_scatter(term, "chip", scatter_dimension=0, tiled=True)
    return summed.astype(jnp.bfloat16)


LANES = 128
MESH = pl.DeviceIdType.MESH
TILES = (5, 7, 9, 7)
PIECES = (6, 12, 10)


def fused_kernel(
    tokens_ref, ids_ref, gates_ref, up_hbm, down_hbm, out_ref,
    ids_v, gates_v, up_v, down_v, gath, rows_v, acc, hid_v, total,
    rows_n, hid_n, side_in, near_total, near_core_out, near_core_in, near_plane_out, near_plane_in,
    core_out, core_in, one_out, one_in, two_out, two_in, near_out, near_in,
    local_sem, up_sem, down_sem, send_sem, recv_sem,
):
    f32, bf16 = jnp.float32, jnp.bfloat16
    node, x = lax.axis_index("node"), lax.axis_index("chip")
    c = lax.rem(node, 2)
    y = lax.rem(lax.div(node, 2), 2)
    z = lax.div(node, 4)
    nz = 4
    tok, model = tokens_ref.shape
    per_node, _, width = up_v.shape
    group = 4 * nz
    half = group * tok

    def dev(zz, yy, cc, xx):
        return ((zz * 2 + yy) * 2 + cc, xx)

    def block(cc, xx, yy, zz):
        return ((cc * 2 + xx) * 2 + yy) * nz + zz

    z_at = [z, z + 1 - 2 * lax.rem(z, 2), lax.rem(z + 2, nz), nz - 1 - z]
    plane_at = [(x, y), (1 - x, y), (x, 1 - y), (1 - x, 1 - y)]
    z_peer = [dev(zz, y, c, x) for zz in z_at]
    z_other = [dev(zz, y, 1 - c, x) for zz in z_at]
    plane_peer = [dev(z, yy, c, xx) for xx, yy in plane_at]
    plane_other = [dev(z, yy, 1 - c, xx) for xx, yy in plane_at]
    c_peer = z_other[0]

    barrier = pltpu.get_barrier_semaphore()
    peers = z_peer[1:] + plane_peer[1:] + z_other + plane_other[1:]
    for peer in peers:
        pl.semaphore_signal(barrier, inc=1, device_id=peer, device_id_type=MESH)

    own = block(c, x, y, z)
    first = TILES[0] * LANES
    parts, begin = {}, 0
    for name, size in zip(("l1", "l2", "l3", "e"), TILES):
        size = size * LANES + (LANES if name == "l2" else 0)
        parts[name] = pl.ds(begin, size)
        begin += size
    local = [
        pltpu.make_async_copy(ids_ref, ids_v, local_sem.at[0]),
        pltpu.make_async_copy(gates_ref, gates_v, local_sem.at[1]),
        pltpu.make_async_copy(
            tokens_ref.at[:, pl.ds(0, first)], gath.at[own, :, pl.ds(0, first)], local_sem.at[2]
        ),
        pltpu.make_async_copy(
            tokens_ref.at[:, pl.ds(first, model - first)],
            gath.at[own, :, pl.ds(first + LANES, model - first)],
            local_sem.at[3],
        ),
    ]
    for copy in local:
        copy.start()
    up_copies = [
        pltpu.make_async_copy(up_hbm.at[e], up_v.at[e], up_sem.at[e]) for e in range(per_node)
    ]
    down_copies = [
        pltpu.make_async_copy(
            down_hbm.at[e], down_v.at[pl.ds(e * width, width)], down_sem.at[e]
        )
        for e in range(per_node)
    ]

    sends = []

    def send(src, dst, peer):
        copy = pltpu.make_async_remote_copy(
            src_ref=src, dst_ref=dst,
            send_sem=send_sem.at[len(sends)], recv_sem=recv_sem.at[len(sends)],
            device_id=peer, device_id_type=MESH,
        )
        copy.start()
        sends.append(copy)
        return copy

    settled = []

    def settle(count):
        for copy in sends[len(settled) : count]:
            copy.wait_send()
            settled.append(copy)

    arriving = {}

    def need(key):
        if key in arriving:
            arriving.pop(key).wait_recv()

    def block_of(g, j):
        return block(c, plane_at[g][0], plane_at[g][1], z_at[j])

    def pass_on(part, source, target, peer):
        ref = gath.at[block_of(*source), :, parts[part]]
        arriving[(part,) + target] = send(ref, ref, peer)

    def own_z(part):
        for j in range(1, nz):
            pass_on(part, (0, 0), (0, j), z_peer[j])

    def own_plane(part, gs=(1, 2, 3)):
        for g in gs:
            pass_on(part, (0, 0), (g, 0), plane_peer[g])

    def z_plane(part, j, gs=(1, 2, 3)):
        need((part, 0, j))
        for g in gs:
            pass_on(part, (0, j), (g, j), plane_peer[g])

    def plane_z(part, g):
        need((part, g, 0))
        for j in range(1, nz):
            pass_on(part, (g, 0), (g, j), z_peer[j])

    def cross(part, j):
        g = 1 + j % 2
        need((part, g, j))
        pass_on(part, (g, j), (3, j), plane_peer[3 - g])

    def gathered(part):
        for g in range(4):
            for j in range(nz):
                need((part, g, j))

    def share(cols):
        ref = gath.at[pl.ds(c * group, group), :, cols]
        return send(ref, ref, c_peer)

    def near_share():
        for part in ("l1", "l2", "l3", "e"):
            for g in range(1, 4):
                need((part, g, 0))
        return [send(gath.at[block_of(g, 0)], side_in.at[g], c_peer) for g in range(4)]

    def near_project(copies):
        tables = []

        def put(row, block_pair):
            pair = block_pair.astype(f32).reshape(2 * tok, model + LANES)
            rows_n[pl.ds(row, 2 * tok), pl.ds(0, first)] = pair[:, :first].astype(bf16)
            rows_n[pl.ds(row, 2 * tok), pl.ds(first, model - first)] = pair[
                :, first + LANES :
            ].astype(bf16)
            tables.append(pair[:, first : first + LANES])

        for g in (0, 2):
            put(g * tok, jnp.stack([gath[block_of(g, 0)], gath[block_of(g + 1, 0)]]))
        for copy in copies:
            copy.wait_recv()
        for g in (0, 2):
            put((4 + g) * tok, side_in[pl.ds(g, 2)])
        table = jnp.concatenate(tables, axis=0)
        lane = lax.broadcasted_iota(jnp.int32, table.shape, 1)
        for e in range(per_node):
            gate = jnp.sum(
                jnp.where(lane == node * per_node + e, table, 0.0), axis=1, keepdims=True
            )
            value = jnp.dot(rows_n[...], up_v[e], preferred_element_type=f32)
            value = (value / (1.0 + jnp.exp(-value))).astype(bf16).astype(f32) * gate
            hid_n[:, pl.ds(e * width, width)] = value.astype(bf16)

    wide = pl.ds(PIECES[0] * LANES, model - PIECES[0] * LANES)

    def near_produce():
        value = jnp.dot(hid_n[...], down_v[:, wide], preferred_element_type=f32)
        value = value.reshape(8, tok, model - PIECES[0] * LANES)
        near_core_out[...] = value[:4].astype(bf16)
        near_total[...] = value[4:]
        return send(near_core_out, near_core_in, c_peer)

    def near_plane(copy):
        copy.wait_recv()
        copies = []
        for g in (3, 1, 2):
            value = near_total[g] + near_core_in[g].astype(f32)
            near_plane_out[g - 1] = value.astype(bf16)
            copies.append(
                send(near_plane_out.at[g - 1], near_plane_in.at[g - 1], plane_peer[g])
            )
        return copies

    def near_last(copies):
        value = near_total[0] + near_core_in[0].astype(f32)
        for copy in copies:
            copy.wait_recv()
        for g in range(3):
            value = value + near_plane_in[g].astype(f32)
        near_out[:, wide] = value
        return send(near_out.at[:, wide], near_in.at[:, wide], c_peer)

    pl.semaphore_wait(barrier, len(peers))
    local[2].wait()
    own_z("l1")
    local[3].wait()
    own_plane("e")
    own_plane("l1")
    local[0].wait()
    local[1].wait()
    table = jnp.zeros((tok, LANES), f32)
    lanes = lax.broadcasted_iota(jnp.int32, (tok, LANES), 1)
    ids = ids_v[...]
    gates = gates_v[...].astype(f32)
    for k in range(ids.shape[1]):
        table = table + jnp.where(ids[:, k : k + 1] == lanes, gates[:, k : k + 1], 0.0)
    gath[own, :, pl.ds(first, LANES)] = table.astype(bf16)
    def weights(side):
        lane = lax.broadcasted_iota(jnp.int32, (half, LANES), 1)
        table = gath[pl.ds(side * group, group), :, pl.ds(first, LANES)]
        table = table.astype(f32).reshape(half, LANES)
        return [
            jnp.sum(jnp.where(lane == node * per_node + e, table, 0.0), axis=1, keepdims=True)
            for e in range(per_node)
        ]

    def project(a, n, sides, weight=None):
        cols = pl.ds(a if a < first else a + LANES, n)
        for side in sides:
            start = (lax.rem(c + side, 2)) * group

            def pack(i, carry):
                pair = gath[pl.ds(start + 2 * i, 2), :, cols].astype(f32)
                row = pl.multiple_of(side * half + 2 * tok * i, 2 * tok)
                rows_v[pl.ds(row, 2 * tok), pl.ds(a, n)] = pair.reshape(2 * tok, n).astype(bf16)
                return carry

            lax.fori_loop(0, group // 2, pack, 0)
        rows = pl.ds(sides[0] * half, len(sides) * half)
        for e in range(per_node):
            value = jnp.dot(
                rows_v[rows, pl.ds(a, n)], up_v[e, pl.ds(a, n)], preferred_element_type=f32
            )
            if a:
                value = value + acc[e, rows]
            if weight is None:
                acc[e, rows] = value
            else:
                value = (value / (1.0 + jnp.exp(-value))).astype(bf16).astype(f32) * weight[e]
                hid_v[rows, pl.ds(e * width, width)] = value.astype(bf16)

    n1, n2 = first, TILES[1] * LANES
    n3 = model - n1 - n2
    own_z("l2")
    own_plane("l2")
    own_z("l3")
    own_plane("l3")
    for copy in up_copies + down_copies:
        copy.start()
    z_plane("l1", 1)
    z_plane("l1", 2)
    z_plane("l1", 3)
    plane_z("e", 1)
    plane_z("e", 2)
    z_plane("l2", 1)
    z_plane("l2", 2)
    z_plane("l2", 3)
    plane_z("e", 3)
    near_copies = near_share()
    z_plane("l3", 1)
    z_plane("l3", 2)
    z_plane("l3", 3)
    own_z("e")

    n1, n2 = first, TILES[1] * LANES
    n3 = model - n1 - n2
    for copy in up_copies:
        copy.wait()
    near_project(near_copies)
    for copy in down_copies:
        copy.wait()
    near_core = near_produce()
    gathered("l1")
    share1 = share(parts["l1"])
    gathered("l2")
    share2 = share(parts["l2"])
    share1.wait_recv()
    project(0, n1, (0, 1))
    share2.wait_recv()
    near_copies = near_plane(near_core)
    project(n1, n2, (0, 1))
    weight = [weights(c), weights(1 - c)]
    gathered("l3")
    gathered("e")
    share3 = share(pl.ds(n1 + n2 + LANES, n3))
    project(n1 + n2, n3, (0,), weight[0])

    count = len(PIECES)
    sizes = [n * LANES for n in PIECES]
    piece_at = [sum(sizes[:q]) for q in range(count)]
    corer, planer, zr = {}, {}, {}

    def span(q):
        return pl.ds(piece_at[q], sizes[q])

    def chips(g):
        return (plane_at[g][0] * 2 + plane_at[g][1]) * nz

    def produce_sent(q):
        value = jnp.dot(hid_v[:half], down_v[:, span(q)], preferred_element_type=f32)
        send_core(q, value)

    def send_core(q, value):
        core_out[:, :, span(q)] = value.reshape(group, tok, sizes[q]).astype(bf16)
        ref = (slice(None), slice(None), span(q))
        corer[q] = send(core_out.at[ref], core_in.at[ref], c_peer)

    def produce_kept(q):
        value = jnp.dot(hid_v[half:], down_v[:, span(q)], preferred_element_type=f32)
        total[:, :, span(q)] = value.reshape(group, tok, sizes[q])

    def produce(q):
        value = jnp.dot(hid_v[...], down_v[:, span(q)], preferred_element_type=f32)
        send_core(q, value[:half])
        total[:, :, span(q)] = value[half:].reshape(group, tok, sizes[q])

    def summed(q, where):
        return total[where, :, span(q)] + core_in[where, :, span(q)].astype(f32)

    def plane_first(q):
        corer[q].wait_recv()
        for g in (3, 1, 2):
            for j in range(1, nz):
                slot = 3 * (g - 1) + j - 1
                one_out[slot, :, span(q)] = summed(q, chips(g) + z_at[j]).astype(bf16)
            ref = (pl.ds(3 * (g - 1), 3), slice(None), span(q))
            planer[q, g] = send(one_out.at[ref], one_in.at[ref], plane_peer[g])

    def plane_then_z(q):
        for g in (1, 2, 3):
            planer[q, g].wait_recv()
        for j in (3, 2, 1):
            value = summed(q, chips(0) + z_at[j])
            for g in range(3):
                value = value + one_in[3 * g + j - 1, :, span(q)].astype(f32)
            two_out[j - 1, :, span(q)] = value.astype(bf16)
            ref = (j - 1, slice(None), span(q))
            zr[q, j] = send(two_out.at[ref], two_in.at[ref], z_other[j])

    def near(q):
        near_out[:, span(q)] = total[chips(0) + z, :, span(q)]
        ref = (slice(None), span(q))
        zr[q, 0] = send(near_out.at[ref], near_in.at[ref], c_peer)

    def z_first(q):
        corer[q].wait_recv()
        for j in (3, 2, 1):
            for g in range(4):
                slot = (j - 1) * 4 + g
                one_out[slot, :, span(q)] = summed(q, chips(g) + z_at[j]).astype(bf16)
            ref = (pl.ds((j - 1) * 4, 4), slice(None), span(q))
            planer[q, j] = send(one_out.at[ref], one_in.at[ref], z_peer[j])

    def z_then_plane(q):
        for j in range(1, nz):
            planer[q, j].wait_recv()
        for g in range(4):
            value = summed(q, chips(g) + z)
            for j in range(1, nz):
                value = value + one_in[(j - 1) * 4 + g, :, span(q)].astype(f32)
            if g == 0:
                total[chips(0) + z, :, span(q)] = value
            else:
                two_out[g - 1, :, span(q)] = value.astype(bf16)
                ref = (g - 1, slice(None), span(q))
                zr[q, g] = send(two_out.at[ref], two_in.at[ref], plane_other[g])
        near(q)

    def finish(q):
        if (q, 0) in zr:
            zr[q, 0].wait_recv()
        value = near_in[:, span(q)]
        for j in range(1, nz):
            zr[q, j].wait_recv()
            value = value + two_in[j - 1, :, span(q)].astype(f32)
        out_ref[:, span(q)] = value.astype(out_ref.dtype)

    gather_count = len(sends)
    produce_sent(1)
    produce_sent(0)
    share3.wait_recv()
    project(n1 + n2, n3, (1,), weight[1])
    produce_kept(1)
    plane_first(1)
    produce_kept(0)
    z_first(0)
    produce(2)
    plane_first(2)
    near_copy = near_last(near_copies)
    settle(gather_count)
    plane_then_z(1)
    z_then_plane(0)
    plane_then_z(2)
    near_copy.wait_recv()
    finish(1)
    finish(0)
    finish(2)
    settle(len(sends))


def fused(tokens, expert_ids, gate_values, up_weight, down_weight):
    tok, model = tokens.shape
    per_node, _, width = up_weight.shape
    bf16, f32 = jnp.bfloat16, jnp.float32
    nz = 4
    group = 4 * nz
    vmem = pl.BlockSpec(memory_space=pltpu.VMEM)
    anyspace = pl.BlockSpec(memory_space=pl.ANY)
    dma = pltpu.SemaphoreType.DMA
    rest = model - PIECES[0] * LANES
    copies = 96
    return pl.pallas_call(
        fused_kernel,
        out_shape=pltpu.VMEM((tok, model), bf16),
        in_specs=[anyspace] * 5,
        out_specs=vmem,
        scratch_shapes=[
            pltpu.VMEM(expert_ids.shape, jnp.int32),
            pltpu.VMEM(gate_values.shape, bf16),
            pltpu.VMEM(up_weight.shape, bf16),
            pltpu.VMEM((per_node * width, model), bf16),
            pltpu.VMEM((2 * group, tok, model + LANES), bf16),
            pltpu.VMEM((2 * group * tok, model), bf16),
            pltpu.VMEM((per_node, 2 * group * tok, width), f32),
            pltpu.VMEM((2 * group * tok, per_node * width), bf16),
            pltpu.VMEM((group, tok, model), f32),
            pltpu.VMEM((8 * tok, model), bf16),
            pltpu.VMEM((8 * tok, per_node * width), bf16),
            pltpu.VMEM((4, tok, model + LANES), bf16),
            pltpu.VMEM((4, tok, rest), f32),
            pltpu.VMEM((4, tok, rest), bf16),
            pltpu.VMEM((4, tok, rest), bf16),
            pltpu.VMEM((3, tok, rest), bf16),
            pltpu.VMEM((3, tok, rest), bf16),
            pltpu.VMEM((group, tok, model), bf16),
            pltpu.VMEM((group, tok, model), bf16),
            pltpu.VMEM((3 * nz, tok, model), bf16),
            pltpu.VMEM((3 * nz, tok, model), bf16),
            pltpu.VMEM((3, tok, model), bf16),
            pltpu.VMEM((3, tok, model), bf16),
            pltpu.VMEM((tok, model), f32),
            pltpu.VMEM((tok, model), f32),
            dma((4,)), dma((per_node,)), dma((per_node,)),
            dma((copies,)), dma((copies,)),
        ],
        compiler_params=pltpu.CompilerParams(
            collective_id=0, has_side_effects=True, vmem_limit_bytes=60 * 1024 * 1024
        ),
    )(tokens, expert_ids, gate_values, up_weight, down_weight)


def body_for(mesh):
    nodes, chips = mesh.shape["node"], mesh.shape["chip"]
    nz = nodes // 4

    def body(tokens, expert_ids, gate_values, slot_ids, up_weight, down_weight):
        tok, model = tokens.shape
        experts = nodes * up_weight.shape[0]
        if (
            chips == 2
            and nodes == 4 * nz
            and nz == 4
            and tok == 8
            and model == sum(TILES) * LANES == sum(PIECES) * LANES
            and experts <= LANES
        ):
            return fused(tokens, expert_ids, gate_values, up_weight, down_weight)
        return shards(tokens, expert_ids, gate_values, slot_ids, up_weight, down_weight)

    return body


def solution(mesh):
    return jax.shard_map(
        body_for(mesh),
        mesh=mesh,
        in_specs=(
            P(("node", "chip"), None),
            P(("node", "chip"), None),
            P(("node", "chip"), None),
            P(("node", "chip"), None),
            P("node", None, "chip"),
            P("node", "chip", None),
        ),
        out_specs=P(("node", "chip"), None),
        check_vma=False,
    )
```

```python
import functools

import jax
import jax.numpy as jnp
from jax import lax
from jax.experimental import pallas as pl
from jax.experimental.pallas import tpu as pltpu
from jax.sharding import PartitionSpec as P


def pack_rows(targets, experts, node_tokens, node_gates, row_count, per_node):
    row_ids = jnp.arange(row_count, dtype=jnp.int32)
    matches = (targets[None, :, :] == row_ids[:, None, None]).astype(jnp.bfloat16)
    picked = jnp.minimum(jnp.sum(matches.astype(jnp.float32), axis=2), 1.0).astype(jnp.bfloat16)
    packed = jnp.dot(picked, node_tokens, preferred_element_type=jnp.float32).astype(jnp.bfloat16)
    choose = (experts[:, :, None] == jnp.arange(per_node, dtype=jnp.int32)[None, None, :]).astype(
        jnp.bfloat16
    )
    weighted = choose * node_gates[:, :, None]
    gate_rows = jnp.einsum(
        "rtk,tke->re", matches, weighted, preferred_element_type=jnp.float32
    ).astype(jnp.bfloat16)
    return (packed, gate_rows)


def expert_rows(row_block, gate_block, up_local, down_local):
    result = jnp.zeros((row_block.shape[0], down_local.shape[2]), jnp.float32)
    for expert in range(up_local.shape[0]):
        hidden = jax.nn.silu(
            jnp.dot(row_block, up_local[expert], preferred_element_type=jnp.float32)
        ).astype(jnp.bfloat16)
        product = jnp.dot(hidden, down_local[expert], preferred_element_type=jnp.float32)
        result = result + gate_block[:, expert : expert + 1].astype(jnp.float32) * product
    return result.astype(jnp.bfloat16)


def gather_sum(indices, table):
    valid = indices >= 0
    safe = jnp.where(valid, indices, 0).reshape(-1)
    picked = jnp.take(table, safe, axis=0).reshape(
        indices.shape[0], indices.shape[1], table.shape[1]
    )
    return jnp.sum(jnp.where(valid[:, :, None], picked, 0.0), axis=1)


def shards(tokens, expert_ids, gate_values, slot_ids, up_weight, down_weight):
    node_count = lax.axis_size("node")
    chip_count = lax.axis_size("chip")
    my_chip = lax.axis_index("chip")
    tok_dev = tokens.shape[0]
    model_dim = tokens.shape[1]
    per_node = up_weight.shape[0]
    capacity = 8 * chip_count * tok_dev // node_count
    block_cap = capacity // chip_count
    route_code = (expert_ids // per_node * capacity + slot_ids) * per_node + expert_ids % per_node
    node_tokens, node_gates = (
        lax.all_gather(tokens, "chip", axis=0, tiled=True),
        lax.all_gather(gate_values, "chip", axis=0, tiled=True),
    )
    node_codes = lax.all_gather(route_code, "chip", axis=0, tiled=True)
    node_expert = node_codes % per_node
    node_slot = node_codes // per_node % capacity
    node_dest = node_codes // per_node // capacity
    targets = node_dest * capacity + node_slot
    packed, gate_rows = pack_rows(
        targets, node_expert, node_tokens, node_gates, node_count * capacity, per_node
    )
    shaped = packed.reshape(node_count, chip_count, 1, block_cap, model_dim)
    gate_shaped = gate_rows.reshape(node_count, chip_count, 1, block_cap, per_node)
    arrived, arrived_gates = (
        lax.all_to_all(shaped, "node", split_axis=0, concat_axis=2, tiled=True),
        lax.all_to_all(gate_shaped, "node", split_axis=0, concat_axis=2, tiled=True),
    )
    row_block = arrived.reshape(-1, model_dim)
    gate_block = arrived_gates.reshape(-1, per_node)
    partial_value = expert_rows(row_block, gate_block, up_weight, down_weight)
    pieces = lax.all_to_all(
        partial_value.reshape(chip_count, node_count * block_cap, model_dim),
        "chip",
        split_axis=0,
        concat_axis=0,
        tiled=True,
    )
    slot_sums = jnp.sum(pieces.astype(jnp.float32), axis=0).reshape(
        node_count, block_cap, model_dim
    )
    held = lax.all_to_all(slot_sums, "node", split_axis=0, concat_axis=0, tiled=True).reshape(
        node_count * block_cap, model_dim
    )
    wanted = (node_slot // block_cap == my_chip) & (node_expert == 0)
    indices = jnp.where(wanted, node_dest * block_cap + node_slot % block_cap, -1)
    term = gather_sum(indices, held)
    summed = lax.psum_scatter(term, "chip", scatter_dimension=0, tiled=True)
    return summed.astype(jnp.bfloat16)


LANES = 128
MESH = pl.DeviceIdType.MESH
TILES = (5, 7, 9, 7)
PIECES = (6, 12, 10)


def fused_kernel(
    tokens_ref, ids_ref, gates_ref, up_hbm, down_hbm, out_ref,
    ids_v, gates_v, up_v, down_v, gath, rows_v, acc, hid_v, total,
    rows_n, hid_n, side_in, near_total, near_core_out, near_core_in, near_plane_out, near_plane_in,
    core_out, core_in, one_out, one_in, two_out, two_in, near_out, near_in,
    local_sem, up_sem, down_sem, send_sem, recv_sem,
):
    f32, bf16 = jnp.float32, jnp.bfloat16
    node, x = lax.axis_index("node"), lax.axis_index("chip")
    c = lax.rem(node, 2)
    y = lax.rem(lax.div(node, 2), 2)
    z = lax.div(node, 4)
    nz = 4
    tok, model = tokens_ref.shape
    per_node, _, width = up_v.shape
    group = 4 * nz
    half = group * tok

    def dev(zz, yy, cc, xx):
        return ((zz * 2 + yy) * 2 + cc, xx)

    def block(cc, xx, yy, zz):
        return ((cc * 2 + xx) * 2 + yy) * nz + zz

    z_at = [z, z + 1 - 2 * lax.rem(z, 2), lax.rem(z + 2, nz), nz - 1 - z]
    plane_at = [(x, y), (1 - x, y), (x, 1 - y), (1 - x, 1 - y)]
    z_peer = [dev(zz, y, c, x) for zz in z_at]
    z_other = [dev(zz, y, 1 - c, x) for zz in z_at]
    plane_peer = [dev(z, yy, c, xx) for xx, yy in plane_at]
    plane_other = [dev(z, yy, 1 - c, xx) for xx, yy in plane_at]
    c_peer = z_other[0]

    barrier = pltpu.get_barrier_semaphore()
    peers = z_peer[1:] + plane_peer[1:] + z_other + plane_other[1:]
    for peer in peers:
        pl.semaphore_signal(barrier, inc=1, device_id=peer, device_id_type=MESH)

    own = block(c, x, y, z)
    first = TILES[0] * LANES
    parts, begin = {}, 0
    for name, size in zip(("l1", "l2", "l3", "e"), TILES):
        size = size * LANES + (LANES if name == "l2" else 0)
        parts[name] = pl.ds(begin, size)
        begin += size
    local = [
        pltpu.make_async_copy(ids_ref, ids_v, local_sem.at[0]),
        pltpu.make_async_copy(gates_ref, gates_v, local_sem.at[1]),
        pltpu.make_async_copy(
            tokens_ref.at[:, pl.ds(0, first)], gath.at[own, :, pl.ds(0, first)], local_sem.at[2]
        ),
        pltpu.make_async_copy(
            tokens_ref.at[:, pl.ds(first, model - first)],
            gath.at[own, :, pl.ds(first + LANES, model - first)],
            local_sem.at[3],
        ),
    ]
    for copy in local:
        copy.start()
    up_copies = [
        pltpu.make_async_copy(up_hbm.at[e], up_v.at[e], up_sem.at[e]) for e in range(per_node)
    ]
    down_copies = [
        pltpu.make_async_copy(
            down_hbm.at[e], down_v.at[pl.ds(e * width, width)], down_sem.at[e]
        )
        for e in range(per_node)
    ]

    sends = []

    def send(src, dst, peer):
        copy = pltpu.make_async_remote_copy(
            src_ref=src, dst_ref=dst,
            send_sem=send_sem.at[len(sends)], recv_sem=recv_sem.at[len(sends)],
            device_id=peer, device_id_type=MESH,
        )
        copy.start()
        sends.append(copy)
        return copy

    settled = []

    def settle(count):
        for copy in sends[len(settled) : count]:
            copy.wait_send()
            settled.append(copy)

    arriving = {}

    def need(key):
        if key in arriving:
            arriving.pop(key).wait_recv()

    def block_of(g, j):
        return block(c, plane_at[g][0], plane_at[g][1], z_at[j])

    def pass_on(part, source, target, peer):
        ref = gath.at[block_of(*source), :, parts[part]]
        arriving[(part,) + target] = send(ref, ref, peer)

    def own_z(part):
        for j in range(1, nz):
            pass_on(part, (0, 0), (0, j), z_peer[j])

    def own_plane(part, gs=(1, 2, 3)):
        for g in gs:
            pass_on(part, (0, 0), (g, 0), plane_peer[g])

    def z_plane(part, j, gs=(1, 2, 3)):
        need((part, 0, j))
        for g in gs:
            pass_on(part, (0, j), (g, j), plane_peer[g])

    def plane_z(part, g):
        need((part, g, 0))
        for j in range(1, nz):
            pass_on(part, (g, 0), (g, j), z_peer[j])

    def gathered(part):
        for g in range(4):
            for j in range(nz):
                need((part, g, j))

    def share(cols):
        ref = gath.at[pl.ds(c * group, group), :, cols]
        return send(ref, ref, c_peer)

    def near_share():
        for part in ("l1", "l2", "l3", "e"):
            for g in range(1, 4):
                need((part, g, 0))
        return [send(gath.at[block_of(g, 0)], side_in.at[g], c_peer) for g in range(4)]

    def near_project(copies):
        tables = []

        def put(row, block_pair):
            pair = block_pair.astype(f32).reshape(2 * tok, model + LANES)
            rows_n[pl.ds(row, 2 * tok), pl.ds(0, first)] = pair[:, :first].astype(bf16)
            rows_n[pl.ds(row, 2 * tok), pl.ds(first, model - first)] = pair[
                :, first + LANES :
            ].astype(bf16)
            tables.append(pair[:, first : first + LANES])

        for g in (0, 2):
            put(g * tok, jnp.stack([gath[block_of(g, 0)], gath[block_of(g + 1, 0)]]))
        for copy in copies:
            copy.wait_recv()
        for g in (0, 2):
            put((4 + g) * tok, side_in[pl.ds(g, 2)])
        table = jnp.concatenate(tables, axis=0)
        lane = lax.broadcasted_iota(jnp.int32, table.shape, 1)
        for e in range(per_node):
            gate = jnp.sum(
                jnp.where(lane == node * per_node + e, table, 0.0), axis=1, keepdims=True
            )
            value = jnp.dot(rows_n[...], up_v[e], preferred_element_type=f32)
            value = (value / (1.0 + jnp.exp(-value))).astype(bf16).astype(f32) * gate
            hid_n[:, pl.ds(e * width, width)] = value.astype(bf16)

    wide = pl.ds(PIECES[0] * LANES, model - PIECES[0] * LANES)

    def near_produce():
        value = jnp.dot(hid_n[...], down_v[:, wide], preferred_element_type=f32)
        value = value.reshape(8, tok, model - PIECES[0] * LANES)
        near_core_out[...] = value[:4].astype(bf16)
        near_total[...] = value[4:]
        return send(near_core_out, near_core_in, c_peer)

    def near_plane(copy):
        copy.wait_recv()
        copies = []
        for g in (3, 1, 2):
            value = near_total[g] + near_core_in[g].astype(f32)
            near_plane_out[g - 1] = value.astype(bf16)
            copies.append(
                send(near_plane_out.at[g - 1], near_plane_in.at[g - 1], plane_peer[g])
            )
        return copies

    def near_last(copies):
        value = near_total[0] + near_core_in[0].astype(f32)
        for copy in copies:
            copy.wait_recv()
        for g in range(3):
            value = value + near_plane_in[g].astype(f32)
        near_out[:, wide] = value
        return send(near_out.at[:, wide], near_in.at[:, wide], c_peer)

    pl.semaphore_wait(barrier, len(peers))
    local[2].wait()
    own_z("l1")
    local[3].wait()
    own_plane("e")
    own_plane("l1")
    local[0].wait()
    local[1].wait()
    table = jnp.zeros((tok, LANES), f32)
    lanes = lax.broadcasted_iota(jnp.int32, (tok, LANES), 1)
    ids = ids_v[...]
    gates = gates_v[...].astype(f32)
    for k in range(ids.shape[1]):
        table = table + jnp.where(ids[:, k : k + 1] == lanes, gates[:, k : k + 1], 0.0)
    gath[own, :, pl.ds(first, LANES)] = table.astype(bf16)
    def weights(side):
        lane = lax.broadcasted_iota(jnp.int32, (half, LANES), 1)
        table = gath[pl.ds(side * group, group), :, pl.ds(first, LANES)]
        table = table.astype(f32).reshape(half, LANES)
        return [
            jnp.sum(jnp.where(lane == node * per_node + e, table, 0.0), axis=1, keepdims=True)
            for e in range(per_node)
        ]

    def project(a, n, sides, weight=None):
        cols = pl.ds(a if a < first else a + LANES, n)
        for side in sides:
            start = (lax.rem(c + side, 2)) * group

            def pack(i, carry):
                pair = gath[pl.ds(start + 2 * i, 2), :, cols].astype(f32)
                row = pl.multiple_of(side * half + 2 * tok * i, 2 * tok)
                rows_v[pl.ds(row, 2 * tok), pl.ds(a, n)] = pair.reshape(2 * tok, n).astype(bf16)
                return carry

            lax.fori_loop(0, group // 2, pack, 0)
        rows = pl.ds(sides[0] * half, len(sides) * half)
        for e in range(per_node):
            value = jnp.dot(
                rows_v[rows, pl.ds(a, n)], up_v[e, pl.ds(a, n)], preferred_element_type=f32
            )
            if a:
                value = value + acc[e, rows]
            if weight is None:
                acc[e, rows] = value
            else:
                value = (value / (1.0 + jnp.exp(-value))).astype(bf16).astype(f32) * weight[e]
                hid_v[rows, pl.ds(e * width, width)] = value.astype(bf16)

    own_z("l2")
    own_plane("l2")
    own_z("l3")
    own_plane("l3")
    for copy in up_copies + down_copies:
        copy.start()
    z_plane("l1", 1)
    z_plane("l1", 2)
    z_plane("l1", 3)
    plane_z("e", 1)
    plane_z("e", 2)
    z_plane("l2", 1)
    z_plane("l2", 2)
    z_plane("l2", 3)
    plane_z("e", 3)
    near_copies = near_share()
    z_plane("l3", 1)
    z_plane("l3", 2)
    z_plane("l3", 3)
    own_z("e")

    n1, n2 = first, TILES[1] * LANES
    n3 = model - n1 - n2
    for copy in up_copies:
        copy.wait()
    near_project(near_copies)
    for copy in down_copies:
        copy.wait()
    near_core = near_produce()
    gathered("l1")
    share1 = share(parts["l1"])
    gathered("l2")
    share2 = share(parts["l2"])
    share1.wait_recv()
    project(0, n1, (0, 1))
    share2.wait_recv()
    near_copies = near_plane(near_core)
    project(n1, n2, (0, 1))
    weight = [weights(c), weights(1 - c)]
    gathered("l3")
    gathered("e")
    share3 = share(pl.ds(n1 + n2 + LANES, n3))
    project(n1 + n2, n3, (0,), weight[0])

    count = len(PIECES)
    sizes = [n * LANES for n in PIECES]
    piece_at = [sum(sizes[:q]) for q in range(count)]
    corer, planer, zr = {}, {}, {}

    def span(q):
        return pl.ds(piece_at[q], sizes[q])

    def chips(g):
        return (plane_at[g][0] * 2 + plane_at[g][1]) * nz

    def produce_sent(q):
        value = jnp.dot(hid_v[:half], down_v[:, span(q)], preferred_element_type=f32)
        send_core(q, value)

    def send_core(q, value):
        core_out[:, :, span(q)] = value.reshape(group, tok, sizes[q]).astype(bf16)
        ref = (slice(None), slice(None), span(q))
        corer[q] = send(core_out.at[ref], core_in.at[ref], c_peer)

    def produce_kept(q):
        value = jnp.dot(hid_v[half:], down_v[:, span(q)], preferred_element_type=f32)
        total[:, :, span(q)] = value.reshape(group, tok, sizes[q])

    def produce(q):
        value = jnp.dot(hid_v[...], down_v[:, span(q)], preferred_element_type=f32)
        send_core(q, value[:half])
        total[:, :, span(q)] = value[half:].reshape(group, tok, sizes[q])

    def summed(q, where):
        return total[where, :, span(q)] + core_in[where, :, span(q)].astype(f32)

    def plane_first(q):
        corer[q].wait_recv()
        for g in (3, 1, 2):
            for j in range(1, nz):
                slot = 3 * (g - 1) + j - 1
                one_out[slot, :, span(q)] = summed(q, chips(g) + z_at[j]).astype(bf16)
            ref = (pl.ds(3 * (g - 1), 3), slice(None), span(q))
            planer[q, g] = send(one_out.at[ref], one_in.at[ref], plane_peer[g])

    def plane_then_z(q):
        for g in (1, 2, 3):
            planer[q, g].wait_recv()
        for j in (3, 2, 1):
            value = summed(q, chips(0) + z_at[j])
            for g in range(3):
                value = value + one_in[3 * g + j - 1, :, span(q)].astype(f32)
            two_out[j - 1, :, span(q)] = value.astype(bf16)
            ref = (j - 1, slice(None), span(q))
            zr[q, j] = send(two_out.at[ref], two_in.at[ref], z_other[j])

    def near(q):
        near_out[:, span(q)] = total[chips(0) + z, :, span(q)]
        ref = (slice(None), span(q))
        zr[q, 0] = send(near_out.at[ref], near_in.at[ref], c_peer)

    def z_first(q):
        corer[q].wait_recv()
        for j in (3, 2, 1):
            for g in range(4):
                slot = (j - 1) * 4 + g
                one_out[slot, :, span(q)] = summed(q, chips(g) + z_at[j]).astype(bf16)
            ref = (pl.ds((j - 1) * 4, 4), slice(None), span(q))
            planer[q, j] = send(one_out.at[ref], one_in.at[ref], z_peer[j])

    def z_then_plane(q):
        for j in range(1, nz):
            planer[q, j].wait_recv()
        for g in range(4):
            value = summed(q, chips(g) + z)
            for j in range(1, nz):
                value = value + one_in[(j - 1) * 4 + g, :, span(q)].astype(f32)
            if g == 0:
                total[chips(0) + z, :, span(q)] = value
            else:
                two_out[g - 1, :, span(q)] = value.astype(bf16)
                ref = (g - 1, slice(None), span(q))
                zr[q, g] = send(two_out.at[ref], two_in.at[ref], plane_other[g])
        near(q)

    def finish(q):
        if (q, 0) in zr:
            zr[q, 0].wait_recv()
        value = near_in[:, span(q)]
        for j in range(1, nz):
            zr[q, j].wait_recv()
            value = value + two_in[j - 1, :, span(q)].astype(f32)
        out_ref[:, span(q)] = value.astype(out_ref.dtype)

    gather_count = len(sends)
    produce_sent(1)
    produce_sent(0)
    share3.wait_recv()
    project(n1 + n2, n3, (1,), weight[1])
    produce_kept(1)
    plane_first(1)
    produce_kept(0)
    z_first(0)
    produce(2)
    plane_first(2)
    near_copy = near_last(near_copies)
    plane_then_z(1)
    z_then_plane(0)
    plane_then_z(2)
    settle(gather_count)
    near_copy.wait_recv()
    finish(1)
    finish(0)
    finish(2)
    settle(len(sends))


def fused(tokens, expert_ids, gate_values, up_weight, down_weight):
    tok, model = tokens.shape
    per_node, _, width = up_weight.shape
    bf16, f32 = jnp.bfloat16, jnp.float32
    nz = 4
    group = 4 * nz
    vmem = pl.BlockSpec(memory_space=pltpu.VMEM)
    anyspace = pl.BlockSpec(memory_space=pl.ANY)
    dma = pltpu.SemaphoreType.DMA
    rest = model - PIECES[0] * LANES
    copies = 96
    return pl.pallas_call(
        fused_kernel,
        out_shape=pltpu.VMEM((tok, model), bf16),
        in_specs=[anyspace] * 5,
        out_specs=vmem,
        scratch_shapes=[
            pltpu.VMEM(expert_ids.shape, jnp.int32),
            pltpu.VMEM(gate_values.shape, bf16),
            pltpu.VMEM(up_weight.shape, bf16),
            pltpu.VMEM((per_node * width, model), bf16),
            pltpu.VMEM((2 * group, tok, model + LANES), bf16),
            pltpu.VMEM((2 * group * tok, model), bf16),
            pltpu.VMEM((per_node, 2 * group * tok, width), f32),
            pltpu.VMEM((2 * group * tok, per_node * width), bf16),
            pltpu.VMEM((group, tok, model), f32),
            pltpu.VMEM((8 * tok, model), bf16),
            pltpu.VMEM((8 * tok, per_node * width), bf16),
            pltpu.VMEM((4, tok, model + LANES), bf16),
            pltpu.VMEM((4, tok, rest), f32),
            pltpu.VMEM((4, tok, rest), bf16),
            pltpu.VMEM((4, tok, rest), bf16),
            pltpu.VMEM((3, tok, rest), bf16),
            pltpu.VMEM((3, tok, rest), bf16),
            pltpu.VMEM((group, tok, model), bf16),
            pltpu.VMEM((group, tok, model), bf16),
            pltpu.VMEM((3 * nz, tok, model), bf16),
            pltpu.VMEM((3 * nz, tok, model), bf16),
            pltpu.VMEM((3, tok, model), bf16),
            pltpu.VMEM((3, tok, model), bf16),
            pltpu.VMEM((tok, model), f32),
            pltpu.VMEM((tok, model), f32),
            dma((4,)), dma((per_node,)), dma((per_node,)),
            dma((copies,)), dma((copies,)),
        ],
        compiler_params=pltpu.CompilerParams(
            collective_id=0, has_side_effects=True, vmem_limit_bytes=60 * 1024 * 1024
        ),
    )(tokens, expert_ids, gate_values, up_weight, down_weight)


def body_for(mesh):
    nodes, chips = mesh.shape["node"], mesh.shape["chip"]
    nz = nodes // 4

    def body(tokens, expert_ids, gate_values, slot_ids, up_weight, down_weight):
        tok, model = tokens.shape
        experts = nodes * up_weight.shape[0]
        if (
            chips == 2
            and nodes == 4 * nz
            and nz == 4
            and tok == 8
            and model == sum(TILES) * LANES == sum(PIECES) * LANES
            and experts <= LANES
        ):
            return fused(tokens, expert_ids, gate_values, up_weight, down_weight)
        return shards(tokens, expert_ids, gate_values, slot_ids, up_weight, down_weight)

    return body


def solution(mesh):
    return jax.shard_map(
        body_for(mesh),
        mesh=mesh,
        in_specs=(
            P(("node", "chip"), None),
            P(("node", "chip"), None),
            P(("node", "chip"), None),
            P(("node", "chip"), None),
            P("node", None, "chip"),
            P("node", "chip", None),
        ),
        out_specs=P(("node", "chip"), None),
        check_vma=False,
    )
```

```python
import functools

import jax
import jax.numpy as jnp
from jax import lax
from jax.experimental import pallas as pl
from jax.experimental.pallas import tpu as pltpu
from jax.sharding import PartitionSpec as P


def pack_rows(targets, experts, node_tokens, node_gates, row_count, per_node):
    row_ids = jnp.arange(row_count, dtype=jnp.int32)
    matches = (targets[None, :, :] == row_ids[:, None, None]).astype(jnp.bfloat16)
    picked = jnp.minimum(jnp.sum(matches.astype(jnp.float32), axis=2), 1.0).astype(jnp.bfloat16)
    packed = jnp.dot(picked, node_tokens, preferred_element_type=jnp.float32).astype(jnp.bfloat16)
    choose = (experts[:, :, None] == jnp.arange(per_node, dtype=jnp.int32)[None, None, :]).astype(
        jnp.bfloat16
    )
    weighted = choose * node_gates[:, :, None]
    gate_rows = jnp.einsum(
        "rtk,tke->re", matches, weighted, preferred_element_type=jnp.float32
    ).astype(jnp.bfloat16)
    return (packed, gate_rows)


def expert_rows(row_block, gate_block, up_local, down_local):
    result = jnp.zeros((row_block.shape[0], down_local.shape[2]), jnp.float32)
    for expert in range(up_local.shape[0]):
        hidden = jax.nn.silu(
            jnp.dot(row_block, up_local[expert], preferred_element_type=jnp.float32)
        ).astype(jnp.bfloat16)
        product = jnp.dot(hidden, down_local[expert], preferred_element_type=jnp.float32)
        result = result + gate_block[:, expert : expert + 1].astype(jnp.float32) * product
    return result.astype(jnp.bfloat16)


def gather_sum(indices, table):
    valid = indices >= 0
    safe = jnp.where(valid, indices, 0).reshape(-1)
    picked = jnp.take(table, safe, axis=0).reshape(
        indices.shape[0], indices.shape[1], table.shape[1]
    )
    return jnp.sum(jnp.where(valid[:, :, None], picked, 0.0), axis=1)


def shards(tokens, expert_ids, gate_values, slot_ids, up_weight, down_weight):
    node_count = lax.axis_size("node")
    chip_count = lax.axis_size("chip")
    my_chip = lax.axis_index("chip")
    tok_dev = tokens.shape[0]
    model_dim = tokens.shape[1]
    per_node = up_weight.shape[0]
    capacity = 8 * chip_count * tok_dev // node_count
    block_cap = capacity // chip_count
    route_code = (expert_ids // per_node * capacity + slot_ids) * per_node + expert_ids % per_node
    node_tokens, node_gates = (
        lax.all_gather(tokens, "chip", axis=0, tiled=True),
        lax.all_gather(gate_values, "chip", axis=0, tiled=True),
    )
    node_codes = lax.all_gather(route_code, "chip", axis=0, tiled=True)
    node_expert = node_codes % per_node
    node_slot = node_codes // per_node % capacity
    node_dest = node_codes // per_node // capacity
    targets = node_dest * capacity + node_slot
    packed, gate_rows = pack_rows(
        targets, node_expert, node_tokens, node_gates, node_count * capacity, per_node
    )
    shaped = packed.reshape(node_count, chip_count, 1, block_cap, model_dim)
    gate_shaped = gate_rows.reshape(node_count, chip_count, 1, block_cap, per_node)
    arrived, arrived_gates = (
        lax.all_to_all(shaped, "node", split_axis=0, concat_axis=2, tiled=True),
        lax.all_to_all(gate_shaped, "node", split_axis=0, concat_axis=2, tiled=True),
    )
    row_block = arrived.reshape(-1, model_dim)
    gate_block = arrived_gates.reshape(-1, per_node)
    partial_value = expert_rows(row_block, gate_block, up_weight, down_weight)
    pieces = lax.all_to_all(
        partial_value.reshape(chip_count, node_count * block_cap, model_dim),
        "chip",
        split_axis=0,
        concat_axis=0,
        tiled=True,
    )
    slot_sums = jnp.sum(pieces.astype(jnp.float32), axis=0).reshape(
        node_count, block_cap, model_dim
    )
    held = lax.all_to_all(slot_sums, "node", split_axis=0, concat_axis=0, tiled=True).reshape(
        node_count * block_cap, model_dim
    )
    wanted = (node_slot // block_cap == my_chip) & (node_expert == 0)
    indices = jnp.where(wanted, node_dest * block_cap + node_slot % block_cap, -1)
    term = gather_sum(indices, held)
    summed = lax.psum_scatter(term, "chip", scatter_dimension=0, tiled=True)
    return summed.astype(jnp.bfloat16)


LANES = 128
MESH = pl.DeviceIdType.MESH
TILES = (5, 6, 10, 7)
PIECES = (6, 12, 10)


def fused_kernel(
    tokens_ref, ids_ref, gates_ref, up_hbm, down_hbm, out_ref,
    ids_v, gates_v, up_v, down_v, gath, rows_v, acc, hid_v, total,
    rows_n, hid_n, side_in, near_total, near_core_out, near_core_in, near_plane_out, near_plane_in,
    core_out, core_in, one_out, one_in, two_out, two_in, near_out, near_in,
    local_sem, up_sem, down_sem, send_sem, recv_sem,
):
    f32, bf16 = jnp.float32, jnp.bfloat16
    node, x = lax.axis_index("node"), lax.axis_index("chip")
    c = lax.rem(node, 2)
    y = lax.rem(lax.div(node, 2), 2)
    z = lax.div(node, 4)
    nz = 4
    tok, model = tokens_ref.shape
    per_node, _, width = up_v.shape
    group = 4 * nz
    half = group * tok

    def dev(zz, yy, cc, xx):
        return ((zz * 2 + yy) * 2 + cc, xx)

    def block(cc, xx, yy, zz):
        return ((cc * 2 + xx) * 2 + yy) * nz + zz

    z_at = [z, z + 1 - 2 * lax.rem(z, 2), lax.rem(z + 2, nz), nz - 1 - z]
    plane_at = [(x, y), (1 - x, y), (x, 1 - y), (1 - x, 1 - y)]
    z_peer = [dev(zz, y, c, x) for zz in z_at]
    z_other = [dev(zz, y, 1 - c, x) for zz in z_at]
    plane_peer = [dev(z, yy, c, xx) for xx, yy in plane_at]
    plane_other = [dev(z, yy, 1 - c, xx) for xx, yy in plane_at]
    c_peer = z_other[0]

    barrier = pltpu.get_barrier_semaphore()
    peers = z_peer[1:] + plane_peer[1:] + z_other + plane_other[1:]
    for peer in peers:
        pl.semaphore_signal(barrier, inc=1, device_id=peer, device_id_type=MESH)

    own = block(c, x, y, z)
    first = TILES[0] * LANES
    parts, begin = {}, 0
    for name, size in zip(("l1", "l2", "l3", "e"), TILES):
        size = size * LANES + (LANES if name == "l2" else 0)
        parts[name] = pl.ds(begin, size)
        begin += size
    local = [
        pltpu.make_async_copy(ids_ref, ids_v, local_sem.at[0]),
        pltpu.make_async_copy(gates_ref, gates_v, local_sem.at[1]),
        pltpu.make_async_copy(
            tokens_ref.at[:, pl.ds(0, first)], gath.at[own, :, pl.ds(0, first)], local_sem.at[2]
        ),
        pltpu.make_async_copy(
            tokens_ref.at[:, pl.ds(first, model - first)],
            gath.at[own, :, pl.ds(first + LANES, model - first)],
            local_sem.at[3],
        ),
    ]
    for copy in local:
        copy.start()
    up_copies = [
        pltpu.make_async_copy(up_hbm.at[e], up_v.at[e], up_sem.at[e]) for e in range(per_node)
    ]
    down_copies = [
        pltpu.make_async_copy(
            down_hbm.at[e], down_v.at[pl.ds(e * width, width)], down_sem.at[e]
        )
        for e in range(per_node)
    ]

    sends = []

    def send(src, dst, peer):
        copy = pltpu.make_async_remote_copy(
            src_ref=src, dst_ref=dst,
            send_sem=send_sem.at[len(sends)], recv_sem=recv_sem.at[len(sends)],
            device_id=peer, device_id_type=MESH,
        )
        copy.start()
        sends.append(copy)
        return copy

    settled = []

    def settle(count):
        for copy in sends[len(settled) : count]:
            copy.wait_send()
            settled.append(copy)

    arriving = {}

    def need(key):
        if key in arriving:
            arriving.pop(key).wait_recv()

    def block_of(g, j):
        return block(c, plane_at[g][0], plane_at[g][1], z_at[j])

    def pass_on(part, source, target, peer):
        ref = gath.at[block_of(*source), :, parts[part]]
        arriving[(part,) + target] = send(ref, ref, peer)

    def own_z(part):
        for j in range(1, nz):
            pass_on(part, (0, 0), (0, j), z_peer[j])

    def own_plane(part, gs=(1, 2, 3)):
        for g in gs:
            pass_on(part, (0, 0), (g, 0), plane_peer[g])

    def z_plane(part, j, gs=(1, 2, 3)):
        need((part, 0, j))
        for g in gs:
            pass_on(part, (0, j), (g, j), plane_peer[g])

    def plane_z(part, g):
        need((part, g, 0))
        for j in range(1, nz):
            pass_on(part, (g, 0), (g, j), z_peer[j])

    def gathered(part):
        for g in range(4):
            for j in range(nz):
                need((part, g, j))

    def share(cols):
        ref = gath.at[pl.ds(c * group, group), :, cols]
        return send(ref, ref, c_peer)

    def near_share():
        for part in ("l1", "l2", "l3", "e"):
            for g in range(1, 4):
                need((part, g, 0))
        return [send(gath.at[block_of(g, 0)], side_in.at[g], c_peer) for g in range(4)]

    def near_project(copies):
        tables = []

        def put(row, block_pair):
            pair = block_pair.astype(f32).reshape(2 * tok, model + LANES)
            rows_n[pl.ds(row, 2 * tok), pl.ds(0, first)] = pair[:, :first].astype(bf16)
            rows_n[pl.ds(row, 2 * tok), pl.ds(first, model - first)] = pair[
                :, first + LANES :
            ].astype(bf16)
            tables.append(pair[:, first : first + LANES])

        for g in (0, 2):
            put(g * tok, jnp.stack([gath[block_of(g, 0)], gath[block_of(g + 1, 0)]]))
        for copy in copies:
            copy.wait_recv()
        for g in (0, 2):
            put((4 + g) * tok, side_in[pl.ds(g, 2)])
        table = jnp.concatenate(tables, axis=0)
        lane = lax.broadcasted_iota(jnp.int32, table.shape, 1)
        for e in range(per_node):
            gate = jnp.sum(
                jnp.where(lane == node * per_node + e, table, 0.0), axis=1, keepdims=True
            )
            value = jnp.dot(rows_n[...], up_v[e], preferred_element_type=f32)
            value = (value / (1.0 + jnp.exp(-value))).astype(bf16).astype(f32) * gate
            hid_n[:, pl.ds(e * width, width)] = value.astype(bf16)

    wide = pl.ds(PIECES[0] * LANES, model - PIECES[0] * LANES)

    def near_produce():
        value = jnp.dot(hid_n[...], down_v[:, wide], preferred_element_type=f32)
        value = value.reshape(8, tok, model - PIECES[0] * LANES)
        near_core_out[...] = value[:4].astype(bf16)
        near_total[...] = value[4:]
        return send(near_core_out, near_core_in, c_peer)

    def near_plane(copy):
        copy.wait_recv()
        copies = []
        for g in (3, 1, 2):
            value = near_total[g] + near_core_in[g].astype(f32)
            near_plane_out[g - 1] = value.astype(bf16)
            copies.append(
                send(near_plane_out.at[g - 1], near_plane_in.at[g - 1], plane_peer[g])
            )
        return copies

    def near_last(copies):
        value = near_total[0] + near_core_in[0].astype(f32)
        for copy in copies:
            copy.wait_recv()
        for g in range(3):
            value = value + near_plane_in[g].astype(f32)
        near_out[:, wide] = value
        return send(near_out.at[:, wide], near_in.at[:, wide], c_peer)

    pl.semaphore_wait(barrier, len(peers))
    local[2].wait()
    own_z("l1")
    local[3].wait()
    own_plane("e")
    own_plane("l1")
    local[0].wait()
    local[1].wait()
    table = jnp.zeros((tok, LANES), f32)
    lanes = lax.broadcasted_iota(jnp.int32, (tok, LANES), 1)
    ids = ids_v[...]
    gates = gates_v[...].astype(f32)
    for k in range(ids.shape[1]):
        table = table + jnp.where(ids[:, k : k + 1] == lanes, gates[:, k : k + 1], 0.0)
    gath[own, :, pl.ds(first, LANES)] = table.astype(bf16)
    def weights(side):
        lane = lax.broadcasted_iota(jnp.int32, (half, LANES), 1)
        table = gath[pl.ds(side * group, group), :, pl.ds(first, LANES)]
        table = table.astype(f32).reshape(half, LANES)
        return [
            jnp.sum(jnp.where(lane == node * per_node + e, table, 0.0), axis=1, keepdims=True)
            for e in range(per_node)
        ]

    def project(a, n, sides, weight=None):
        cols = pl.ds(a if a < first else a + LANES, n)
        for side in sides:
            start = (lax.rem(c + side, 2)) * group

            def pack(i, carry):
                pair = gath[pl.ds(start + 2 * i, 2), :, cols].astype(f32)
                row = pl.multiple_of(side * half + 2 * tok * i, 2 * tok)
                rows_v[pl.ds(row, 2 * tok), pl.ds(a, n)] = pair.reshape(2 * tok, n).astype(bf16)
                return carry

            lax.fori_loop(0, group // 2, pack, 0)
        rows = pl.ds(sides[0] * half, len(sides) * half)
        for e in range(per_node):
            value = jnp.dot(
                rows_v[rows, pl.ds(a, n)], up_v[e, pl.ds(a, n)], preferred_element_type=f32
            )
            if a:
                value = value + acc[e, rows]
            if weight is None:
                acc[e, rows] = value
            else:
                value = (value / (1.0 + jnp.exp(-value))).astype(bf16).astype(f32) * weight[e]
                hid_v[rows, pl.ds(e * width, width)] = value.astype(bf16)

    own_z("l2")
    own_plane("l2")
    own_z("l3")
    own_plane("l3")
    for copy in up_copies + down_copies:
        copy.start()
    z_plane("l1", 1)
    z_plane("l1", 2)
    z_plane("l1", 3)
    plane_z("e", 1)
    plane_z("e", 2)
    z_plane("l2", 1)
    z_plane("l2", 2)
    z_plane("l2", 3)
    plane_z("e", 3)
    own_z("e")
    near_copies = near_share()
    z_plane("l3", 1)
    z_plane("l3", 2)
    z_plane("l3", 3)

    n1, n2 = first, TILES[1] * LANES
    n3 = model - n1 - n2
    for copy in up_copies:
        copy.wait()
    near_project(near_copies)
    for copy in down_copies:
        copy.wait()
    near_core = near_produce()
    gathered("l1")
    share1 = share(parts["l1"])
    gathered("l2")
    share2 = share(parts["l2"])
    share1.wait_recv()
    project(0, n1, (0, 1))
    share2.wait_recv()
    near_copies = near_plane(near_core)
    project(n1, n2, (0, 1))
    weight = [weights(c), weights(1 - c)]
    gathered("l3")
    gathered("e")
    share3 = share(pl.ds(n1 + n2 + LANES, n3))
    project(n1 + n2, n3, (0,), weight[0])

    count = len(PIECES)
    sizes = [n * LANES for n in PIECES]
    piece_at = [sum(sizes[:q]) for q in range(count)]
    corer, planer, zr = {}, {}, {}

    def span(q):
        return pl.ds(piece_at[q], sizes[q])

    def chips(g):
        return (plane_at[g][0] * 2 + plane_at[g][1]) * nz

    def produce_sent(q):
        value = jnp.dot(hid_v[:half], down_v[:, span(q)], preferred_element_type=f32)
        send_core(q, value)

    def send_core(q, value):
        core_out[:, :, span(q)] = value.reshape(group, tok, sizes[q]).astype(bf16)
        ref = (slice(None), slice(None), span(q))
        corer[q] = send(core_out.at[ref], core_in.at[ref], c_peer)

    def produce_kept(q):
        value = jnp.dot(hid_v[half:], down_v[:, span(q)], preferred_element_type=f32)
        total[:, :, span(q)] = value.reshape(group, tok, sizes[q])

    def produce(q):
        value = jnp.dot(hid_v[...], down_v[:, span(q)], preferred_element_type=f32)
        send_core(q, value[:half])
        total[:, :, span(q)] = value[half:].reshape(group, tok, sizes[q])

    def summed(q, where):
        return total[where, :, span(q)] + core_in[where, :, span(q)].astype(f32)

    def plane_first(q):
        corer[q].wait_recv()
        for g in (3, 1, 2):
            for j in range(1, nz):
                slot = 3 * (g - 1) + j - 1
                one_out[slot, :, span(q)] = summed(q, chips(g) + z_at[j]).astype(bf16)
            ref = (pl.ds(3 * (g - 1), 3), slice(None), span(q))
            planer[q, g] = send(one_out.at[ref], one_in.at[ref], plane_peer[g])

    def plane_then_z(q):
        for g in (1, 2, 3):
            planer[q, g].wait_recv()
        for j in (3, 2, 1):
            value = summed(q, chips(0) + z_at[j])
            for g in range(3):
                value = value + one_in[3 * g + j - 1, :, span(q)].astype(f32)
            two_out[j - 1, :, span(q)] = value.astype(bf16)
            ref = (j - 1, slice(None), span(q))
            zr[q, j] = send(two_out.at[ref], two_in.at[ref], z_other[j])

    def near(q):
        near_out[:, span(q)] = total[chips(0) + z, :, span(q)]
        ref = (slice(None), span(q))
        zr[q, 0] = send(near_out.at[ref], near_in.at[ref], c_peer)

    def z_first(q):
        corer[q].wait_recv()
        for j in (3, 2, 1):
            for g in range(4):
                slot = (j - 1) * 4 + g
                one_out[slot, :, span(q)] = summed(q, chips(g) + z_at[j]).astype(bf16)
            ref = (pl.ds((j - 1) * 4, 4), slice(None), span(q))
            planer[q, j] = send(one_out.at[ref], one_in.at[ref], z_peer[j])

    def z_then_plane(q):
        for j in range(1, nz):
            planer[q, j].wait_recv()
        for g in range(4):
            value = summed(q, chips(g) + z)
            for j in range(1, nz):
                value = value + one_in[(j - 1) * 4 + g, :, span(q)].astype(f32)
            if g == 0:
                total[chips(0) + z, :, span(q)] = value
            else:
                two_out[g - 1, :, span(q)] = value.astype(bf16)
                ref = (g - 1, slice(None), span(q))
                zr[q, g] = send(two_out.at[ref], two_in.at[ref], plane_other[g])
        near(q)

    def finish(q):
        if (q, 0) in zr:
            zr[q, 0].wait_recv()
        value = near_in[:, span(q)]
        for j in range(1, nz):
            zr[q, j].wait_recv()
            value = value + two_in[j - 1, :, span(q)].astype(f32)
        out_ref[:, span(q)] = value.astype(out_ref.dtype)

    gather_count = len(sends)
    produce_sent(1)
    produce_sent(0)
    share3.wait_recv()
    project(n1 + n2, n3, (1,), weight[1])
    produce_kept(1)
    plane_first(1)
    produce_kept(0)
    z_first(0)
    produce(2)
    plane_first(2)
    near_copy = near_last(near_copies)
    plane_then_z(1)
    z_then_plane(0)
    plane_then_z(2)
    settle(gather_count)
    near_copy.wait_recv()
    finish(1)
    finish(0)
    finish(2)
    settle(len(sends))


def fused(tokens, expert_ids, gate_values, up_weight, down_weight):
    tok, model = tokens.shape
    per_node, _, width = up_weight.shape
    bf16, f32 = jnp.bfloat16, jnp.float32
    nz = 4
    group = 4 * nz
    vmem = pl.BlockSpec(memory_space=pltpu.VMEM)
    anyspace = pl.BlockSpec(memory_space=pl.ANY)
    dma = pltpu.SemaphoreType.DMA
    rest = model - PIECES[0] * LANES
    copies = 96
    return pl.pallas_call(
        fused_kernel,
        out_shape=pltpu.VMEM((tok, model), bf16),
        in_specs=[anyspace] * 5,
        out_specs=vmem,
        scratch_shapes=[
            pltpu.VMEM(expert_ids.shape, jnp.int32),
            pltpu.VMEM(gate_values.shape, bf16),
            pltpu.VMEM(up_weight.shape, bf16),
            pltpu.VMEM((per_node * width, model), bf16),
            pltpu.VMEM((2 * group, tok, model + LANES), bf16),
            pltpu.VMEM((2 * group * tok, model), bf16),
            pltpu.VMEM((per_node, 2 * group * tok, width), f32),
            pltpu.VMEM((2 * group * tok, per_node * width), bf16),
            pltpu.VMEM((group, tok, model), f32),
            pltpu.VMEM((8 * tok, model), bf16),
            pltpu.VMEM((8 * tok, per_node * width), bf16),
            pltpu.VMEM((4, tok, model + LANES), bf16),
            pltpu.VMEM((4, tok, rest), f32),
            pltpu.VMEM((4, tok, rest), bf16),
            pltpu.VMEM((4, tok, rest), bf16),
            pltpu.VMEM((3, tok, rest), bf16),
            pltpu.VMEM((3, tok, rest), bf16),
            pltpu.VMEM((group, tok, model), bf16),
            pltpu.VMEM((group, tok, model), bf16),
            pltpu.VMEM((3 * nz, tok, model), bf16),
            pltpu.VMEM((3 * nz, tok, model), bf16),
            pltpu.VMEM((3, tok, model), bf16),
            pltpu.VMEM((3, tok, model), bf16),
            pltpu.VMEM((tok, model), f32),
            pltpu.VMEM((tok, model), f32),
            dma((4,)), dma((per_node,)), dma((per_node,)),
            dma((copies,)), dma((copies,)),
        ],
        compiler_params=pltpu.CompilerParams(
            collective_id=0, has_side_effects=True, vmem_limit_bytes=60 * 1024 * 1024
        ),
    )(tokens, expert_ids, gate_values, up_weight, down_weight)


def body_for(mesh):
    nodes, chips = mesh.shape["node"], mesh.shape["chip"]
    nz = nodes // 4

    def body(tokens, expert_ids, gate_values, slot_ids, up_weight, down_weight):
        tok, model = tokens.shape
        experts = nodes * up_weight.shape[0]
        if (
            chips == 2
            and nodes == 4 * nz
            and nz == 4
            and tok == 8
            and model == sum(TILES) * LANES == sum(PIECES) * LANES
            and experts <= LANES
        ):
            return fused(tokens, expert_ids, gate_values, up_weight, down_weight)
        return shards(tokens, expert_ids, gate_values, slot_ids, up_weight, down_weight)

    return body


def solution(mesh):
    return jax.shard_map(
        body_for(mesh),
        mesh=mesh,
        in_specs=(
            P(("node", "chip"), None),
            P(("node", "chip"), None),
            P(("node", "chip"), None),
            P(("node", "chip"), None),
            P("node", None, "chip"),
            P("node", "chip", None),
        ),
        out_specs=P(("node", "chip"), None),
        check_vma=False,
    )
```
